256 devices in a mesh: blk: 16 (over z, x_hi), leaf: 8 (over y, core), rhs: 2 (over x_lo).
Axes of the slice: x: 4 (x_hi: 2, x_lo: 2; x = x_hi * 2 + x_lo), y: 4, z: 8, core: 2. Of those that a mesh axis runs over, the one named last changes fastest.
Arguments:
- residual: float32 [32, 8, 65536], P('rhs', 'leaf', 'blk'), may hold values from -160 to 160
- points: float32 [3, 8, 65536], P(None, 'leaf', 'blk'), may hold values from -12330 to 12330
- noise: float32 [8, 65536], P('leaf', 'blk'), may hold values from 1 to 2
- block_list: int32 [8, 8, 256], P('leaf'), may hold values from 0 to 1, as said below
Outputs:
- correction: float32 [32, 8, 65536], P('rhs', 'leaf', 'blk')
- new_residual: float32 [32, 8, 65536], P('rhs', 'leaf', 'blk')
- basis: float32 [128, 8, 65536], P('rhs', 'leaf', 'blk')
The draws below stay inside these ranges and needn't reach their ends.
Inputs may be any that keep to these rules, and one draw needn't show every extreme that they name: The list is symmetric: block_list[t, k, i] == block_list[t, 7 - k, (i + d) mod 256] with d the offset of entry k.
All inputs are finite; a program needn't handle non-finite values.
Results may differ from the reference program's by a relative error of at most 0.007.
Values sent between devices are 32-bit elements; how exact they have to be, the bound alone decides.
A program may use at most 128 MiB of HBM per device.

```python
import math
import jax
import jax.numpy as jnp
from jax import lax

M = 32
S = 4
BS = 256
REACH = 4
SUPPORT = 1408
LOOP_BLKS = 256
LOOP_PTS = 65536
LOOPS = 8


def draw_residual(key, part):
    keys = jax.random.split(key, 6)
    position = jnp.arange(LOOP_PTS, dtype=jnp.float32) / LOOP_PTS
    trend = 1.0 + 2.0 * position
    angle = jnp.arange(LOOP_PTS, dtype=jnp.float32) * (2.0 * math.pi / LOOP_PTS)
    harmonics = [max(1, LOOP_PTS // (spread * SUPPORT)) for spread in (2, 3, 5, 8)]
    phases = jax.random.uniform(keys[4], (4, M, LOOPS, 1), jnp.float32, 0.0, 2.0 * math.pi)
    amounts = 2.0 * jnp.clip(jax.random.normal(keys[5], (4, M, LOOPS, 1), jnp.float32), -3.0, 3.0)
    smooth = sum((amounts[j] * jnp.sin(harmonics[j] * angle + phases[j]) for j in range(4)))
    base = jnp.clip(jax.random.normal(keys[0], (M, LOOPS, LOOP_PTS), jnp.float32), -4.0, 4.0)
    row_scale = jnp.exp(jax.random.uniform(keys[1], (LOOPS, LOOP_PTS), jnp.float32, 0.0, 1.2))
    column_scale = jnp.exp(jax.random.uniform(keys[2], (M, 1, 1), jnp.float32, 0.0, 1.2))
    return (smooth + base * row_scale[None]) * trend * column_scale / 3.0


def draw_points(key, part):
    keys = jax.random.split(key, 5)
    jitter = jax.random.uniform(keys[0], (LOOPS, LOOP_PTS), jnp.float32, 0.0, 0.9)
    along = jnp.arange(LOOP_PTS, dtype=jnp.float32)[None] + jitter
    angle = along * (2.0 * math.pi / LOOP_PTS)
    centre = LOOP_PTS / (2.0 * math.pi)
    reach = 0.06 * SUPPORT
    radial = jax.random.uniform(keys[1], (LOOPS, LOOP_PTS), jnp.float32, -reach, reach)
    height = jax.random.uniform(keys[2], (LOOPS, LOOP_PTS), jnp.float32, -reach, reach)
    radius = centre + radial
    return jnp.stack([radius * jnp.cos(angle), radius * jnp.sin(angle), height], axis=0)


def draw_block_list(key, part):
    upper = (jax.random.randint(key, (LOOPS, REACH, LOOP_BLKS), 0, 4) > 0).astype(jnp.int32)
    lower = [jnp.roll(upper[:, offset - 1], offset, axis=-1) for offset in range(REACH, 0, -1)]
    return jnp.concatenate([jnp.stack(lower, axis=1), upper], axis=1)


def levels(rng, dims, cuts, least, high):
    def one(dim, blocks):
        steps = jax.random.uniform(jax.random.fold_in(jax.random.fold_in(rng, 6), dim), (blocks,), jnp.float32, least / len(cuts), high / len(cuts))
        return jnp.repeat(jnp.exp(steps), dims[dim] // blocks).reshape((-1,) + (1,) * (len(dims) - dim - 1))

    loudness = one(*cuts[0])
    for cut in cuts[1:]:
        loudness = loudness * one(*cut)
    return loudness


def setup_inputs(seed: int = 0) -> dict:
    key_list = jax.random.split(jax.random.key(seed), 5)
    return {
        "residual": draw_residual(jax.random.fold_in(key_list[4], 71), 0),
        "points": draw_points(jax.random.fold_in(key_list[4], 71), 0),
        "noise": jnp.clip(1.0 + 1.0 * jax.random.uniform(key_list[2], (LOOPS, LOOP_PTS), jnp.float32) ** levels(key_list[2], (LOOPS, LOOP_PTS), ((0, 8), (1, 16)), -0.2, 0.2), 1.0, 2.0),
        "block_list": draw_block_list(jax.random.fold_in(key_list[4], 71), 0),
    }


centre_shift = 1.5
amplitude = 1.1
exact = lax.Precision.HIGHEST

def kernel_tile(near_points, own_points):
    squared = (near_points[0][:, None] - own_points[0][None, :]) ** 2
    squared = squared + (near_points[1][:, None] - own_points[1][None, :]) ** 2
    squared = squared + (near_points[2][:, None] - own_points[2][None, :]) ** 2
    radius = jnp.sqrt(squared) / SUPPORT
    remain = jnp.maximum(1.0 - radius, 0.0)
    return remain * remain * (remain * remain) * (4.0 * radius + 1.0) * (amplitude / SUPPORT)

def shifted_operator(field, points, noise, listed):
    blocks = LOOP_PTS // BS
    width = 2 * REACH + 1
    field_blocks = field.reshape(M, LOOPS, blocks, BS)
    point_blocks = points.reshape(3, LOOPS, blocks, BS)
    nine = jnp.concatenate([listed[:, :REACH], jnp.ones((LOOPS, 1, blocks), jnp.float32), listed[:, REACH:]], axis=1)
    field_wide = jnp.concatenate([field_blocks[:, :, -REACH:], field_blocks, field_blocks[:, :, :REACH]], axis=2)
    point_wide = jnp.concatenate([point_blocks[:, :, -REACH:], point_blocks, point_blocks[:, :, :REACH]], axis=2)

    def one_row(index):
        track = index // blocks
        row = index % blocks
        zero = jnp.zeros((), jnp.int32)
        own_points = lax.dynamic_slice(point_wide, (zero, track, row + REACH, zero), (3, 1, 1, BS))[:, 0, 0]
        near_points = lax.dynamic_slice(point_wide, (zero, track, row, zero), (3, 1, width, BS))[:, 0]
        near_field = lax.dynamic_slice(field_wide, (zero, track, row, zero), (M, 1, width, BS))[:, 0]
        weights = lax.dynamic_slice(nine, (track, zero, row), (1, width, 1))[0, :, 0]
        tiles = jax.vmap(kernel_tile, in_axes=(1, None))(near_points, own_points)
        tiles = tiles * weights[:, None, None]
        return jnp.einsum('mkq,kqp->mp', near_field, tiles, precision=exact)
    rows = lax.map(one_row, jnp.arange(LOOPS * blocks, dtype=jnp.int32))
    kernel_part = jnp.moveaxis(rows.reshape(LOOPS, blocks, M, BS), 2, 0).reshape(M, LOOPS, LOOP_PTS)
    return kernel_part + (noise[None] - centre_shift) * field

def galerkin(gram, count_points, count_sides):
    normed = gram / count_points
    basis_count = normed.shape[0] - count_sides
    gram_basis = normed[:basis_count, :basis_count]
    factor_low = jnp.linalg.cholesky(gram_basis)
    inverse_low = lax.linalg.triangular_solve(factor_low, jnp.eye(basis_count, dtype=jnp.float32), left_side=True, lower=True)
    cross = normed[:basis_count, count_sides:] + centre_shift * gram_basis
    projected = jnp.dot(jnp.dot(inverse_low, cross, precision=exact), inverse_low.T, precision=exact)
    projected = 0.5 * (projected + projected.T)
    small_side = jnp.dot(inverse_low, gram_basis[:, :count_sides], precision=exact)
    proj_factor = jnp.linalg.cholesky(projected)
    halfway = lax.linalg.triangular_solve(proj_factor, small_side, left_side=True, lower=True)
    coeffs = lax.linalg.triangular_solve(proj_factor, halfway, left_side=True, lower=True, transpose_a=True)
    combo = jnp.dot(coeffs.T, inverse_low, precision=exact)
    return (inverse_low, combo)

def reference(residual, points, noise, block_list):
    listed = block_list.astype(jnp.float32)
    powers = [residual]
    for power_step in range(S):
        powers.append(shifted_operator(powers[-1], points, noise, listed))
    panel = jnp.stack(powers, 0).reshape((S + 1) * M, LOOPS * LOOP_PTS)
    gram = jnp.dot(panel, panel.T, precision=exact)
    inverse_low, combo = galerkin(gram, LOOPS * LOOP_PTS, M)
    first_rows = panel[:S * M]
    image = panel[M:] + centre_shift * first_rows
    correction = jnp.dot(combo, first_rows, precision=exact)
    new_residual = panel[:M] - jnp.dot(combo, image, precision=exact)
    basis = jnp.dot(inverse_low, first_rows, precision=exact)
    return (correction.reshape(M, LOOPS, LOOP_PTS), new_residual.reshape(M, LOOPS, LOOP_PTS), basis.reshape(S * M, LOOPS, LOOP_PTS))
```

```python
import jax
import jax.numpy as jnp
from jax import lax
from jax.sharding import PartitionSpec as P

M = 32
S = 4
BS = 256
REACH = 4
SUPPORT = 1408


centre_shift = 1.5
amplitude = 1.1
exact = lax.Precision.HIGHEST


def extended(x, sides, width):
    for axis, dim in sides:
        count, length = (lax.axis_size(axis), x.shape[dim])
        up = [(i, (i + 1) % count) for i in range(count)]
        down = [(j, i) for i, j in up]
        last = lax.slice_in_dim(x, length - width, length, axis=dim)
        leading = lax.slice_in_dim(x, 0, width, axis=dim)
        before = lax.ppermute(last, axis, up)
        after = lax.ppermute(leading, axis, down)
        x = jnp.concatenate([before, x, after], axis=dim)
    return x


def kernel_tile(near_points, own_points):
    squared = (near_points[0][:, None] - own_points[0][None, :]) ** 2
    squared = squared + (near_points[1][:, None] - own_points[1][None, :]) ** 2
    squared = squared + (near_points[2][:, None] - own_points[2][None, :]) ** 2
    radius = jnp.sqrt(squared) / SUPPORT
    remain = jnp.maximum(1.0 - radius, 0.0)
    return remain * remain * (remain * remain) * (4.0 * radius + 1.0) * (amplitude / SUPPORT)


def band_product(field_wide, points_wide, weights, rows_out):
    per_turn = rows_out // 8
    count = field_wide.shape[0]

    def turn(carry, index):
        pieces = []
        for inner in range(per_turn):
            block = index * per_turn + inner
            own_points = lax.dynamic_slice_in_dim(points_wide, (block + REACH) * BS, BS, 1)
            total = jnp.zeros((count, BS), jnp.float32)
            for offset in range(2 * REACH + 1):
                column_at = (block + offset) * BS
                near_points = lax.dynamic_slice_in_dim(points_wide, column_at, BS, 1)
                near_field = lax.dynamic_slice_in_dim(field_wide, column_at, BS, 1)
                listed = lax.dynamic_index_in_dim(weights[offset], block, 0, False)
                tile = kernel_tile(near_points, own_points) * listed
                total = total + jnp.dot(near_field, tile, precision=exact)
            pieces.append(total)
        return (carry, jnp.concatenate(pieces, axis=1))

    carry, parts = lax.scan(turn, jnp.zeros((), jnp.int32), jnp.arange(8, dtype=jnp.int32))
    return jnp.moveaxis(parts, 0, 1).reshape(count, rows_out * BS)


def galerkin(gram, count_points, count_sides):
    normed = gram / count_points
    basis_count = normed.shape[0]
    gram_basis = normed[:basis_count, :basis_count]
    factor_low = jnp.linalg.cholesky(gram_basis)
    inverse_low = lax.linalg.triangular_solve(
        factor_low, jnp.eye(basis_count, dtype=jnp.float32), left_side=True, lower=True
    )
    cross = normed[:basis_count, count_sides:] + centre_shift * gram_basis
    projected = jnp.dot(
        jnp.dot(inverse_low, cross, precision=exact), inverse_low.T, precision=exact
    )
    projected = 0.5 * (projected + projected.T)
    small_side = jnp.dot(inverse_low, gram_basis[:, :count_sides], precision=exact)
    proj_factor = jnp.linalg.cholesky(projected)
    halfway = lax.linalg.triangular_solve(proj_factor, small_side, left_side=True, lower=True)
    coeffs = lax.linalg.triangular_solve(
        proj_factor, halfway, left_side=True, lower=True, transpose_a=True
    )
    combo = jnp.dot(coeffs.T, inverse_low, precision=exact)
    return (inverse_low, combo)


def row_products(rows, cols):
    return lax.dot_general(rows, cols, (((1,), (1,)), ((), ())), precision=exact)


def butterfly_sum(x, axes):
    for axis in axes:
        count = lax.axis_size(axis)
        if count & (count - 1):
            x = lax.psum(x, axis)
            continue
        step = 1
        while step < count:
            x = x + lax.ppermute(x, axis, [(i, i ^ step) for i in range(count)])
            step *= 2
    return x


def local(residual, points, noise, block_list):
    field = residual[:, 0]
    coords = points[:, 0]
    nugget = noise[0]
    own_rows = field.shape[1]
    own_blocks = own_rows // BS
    first_block = lax.axis_index("blk") * own_blocks
    listed = block_list[0].astype(jnp.float32)
    nine = jnp.concatenate(
        [listed[:REACH], jnp.ones((1, listed.shape[1]), jnp.float32), listed[REACH:]], axis=0
    )
    margin = S * REACH
    wrapped = jnp.concatenate([nine[:, -margin:], nine, nine[:, :margin]], axis=1)
    powers = [field]
    rim = REACH * BS
    coords_wide = extended(coords, (("blk", 1),), rim)
    own_weights = lax.dynamic_slice_in_dim(wrapped, first_block + margin, own_blocks, 1)
    current = field
    for power_step in range(S):
        widened = extended(current, (("blk", 1),), rim)
        current = (
            band_product(widened, coords_wide, own_weights, own_blocks)
            + (nugget - centre_shift) * current
        )
        powers.append(current)
    half_panel = jnp.stack(powers, axis=0)
    count_points = own_rows * lax.axis_size("blk") * lax.axis_size("leaf")
    sides_here = field.shape[0]
    whole = lax.all_gather(half_panel, "rhs", axis=1, tiled=True)
    flat = whole.reshape(-1, own_rows)
    gram = butterfly_sum(row_products(flat[: S * M], flat), ("leaf", "blk"))
    inverse_low, combo = galerkin(gram, count_points, M)
    first_rows = flat[: S * M]
    image = flat[M:] + centre_shift * first_rows
    part = lax.axis_index("rhs")
    basis_here = S * M // lax.axis_size("rhs")
    mine_low = lax.dynamic_slice_in_dim(inverse_low, part * basis_here, basis_here, 0)
    mine_combo = lax.dynamic_slice_in_dim(combo, part * sides_here, sides_here, 0)
    correction = jnp.dot(mine_combo, first_rows, precision=exact)
    new_residual = field - jnp.dot(mine_combo, image, precision=exact)
    basis = jnp.dot(mine_low, first_rows, precision=exact)
    return (correction[:, None], new_residual[:, None], basis[:, None])


def solution(mesh):
    placed = (
        P("rhs", "leaf", "blk"),
        P(None, "leaf", "blk"),
        P("leaf", "blk"),
        P("leaf", None, None),
    )
    return jax.shard_map(
        local,
        mesh=mesh,
        in_specs=placed,
        out_specs=(P("rhs", "leaf", "blk"), P("rhs", "leaf", "blk"), P("rhs", "leaf", "blk")),
        check_vma=False,
    )
```

```python
import jax
import jax.numpy as jnp
from jax import lax
from jax.sharding import PartitionSpec as P

M = 32
S = 4
BS = 256
REACH = 4
SUPPORT = 1408


centre_shift = 1.5
amplitude = 1.1
exact = lax.Precision.HIGHEST


def extended(x, sides, width):
    for axis, dim in sides:
        count, length = (lax.axis_size(axis), x.shape[dim])
        up = [(i, (i + 1) % count) for i in range(count)]
        down = [(j, i) for i, j in up]
        last = lax.slice_in_dim(x, length - width, length, axis=dim)
        leading = lax.slice_in_dim(x, 0, width, axis=dim)
        before = lax.ppermute(last, axis, up)
        after = lax.ppermute(leading, axis, down)
        x = jnp.concatenate([before, x, after], axis=dim)
    return x


def kernel_tile(near_points, own_points):
    squared = (near_points[0][:, None] - own_points[0][None, :]) ** 2
    squared = squared + (near_points[1][:, None] - own_points[1][None, :]) ** 2
    squared = squared + (near_points[2][:, None] - own_points[2][None, :]) ** 2
    radius = jnp.sqrt(squared) / SUPPORT
    remain = jnp.maximum(1.0 - radius, 0.0)
    return remain * remain * (remain * remain) * (4.0 * radius + 1.0) * (amplitude / SUPPORT)


def band_tiles(points_wide, weights, rows_out):
    width = 2 * REACH + 1
    blocks = points_wide.reshape(3, -1, BS)
    own = blocks[:, REACH : REACH + rows_out]
    near = jnp.stack([blocks[:, k : k + rows_out] for k in range(width)], axis=2)
    tiles = jax.vmap(jax.vmap(kernel_tile, in_axes=(1, None)), in_axes=(1, 1))(near, own)
    return tiles * jnp.transpose(weights)[:, :, None, None]


def band_product(field_wide, tiles, rows_out):
    width = 2 * REACH + 1
    count = field_wide.shape[0]
    blocks = field_wide.reshape(count, -1, BS)
    near = jnp.stack([blocks[:, k : k + rows_out] for k in range(width)], axis=2)
    out = jnp.einsum("mbkq,bkqp->mbp", near, tiles, precision=exact)
    return out.reshape(count, rows_out * BS)


def galerkin(gram, count_points, count_sides):
    normed = gram / count_points
    basis_count = normed.shape[0]
    gram_basis = normed[:basis_count, :basis_count]
    factor_low = jnp.linalg.cholesky(gram_basis)
    inverse_low = lax.linalg.triangular_solve(
        factor_low, jnp.eye(basis_count, dtype=jnp.float32), left_side=True, lower=True
    )
    cross = normed[:basis_count, count_sides:] + centre_shift * gram_basis
    projected = jnp.dot(
        jnp.dot(inverse_low, cross, precision=exact), inverse_low.T, precision=exact
    )
    projected = 0.5 * (projected + projected.T)
    small_side = jnp.dot(inverse_low, gram_basis[:, :count_sides], precision=exact)
    proj_factor = jnp.linalg.cholesky(projected)
    halfway = lax.linalg.triangular_solve(proj_factor, small_side, left_side=True, lower=True)
    coeffs = lax.linalg.triangular_solve(
        proj_factor, halfway, left_side=True, lower=True, transpose_a=True
    )
    combo = jnp.dot(coeffs.T, inverse_low, precision=exact)
    return (inverse_low, combo)


def row_products(rows, cols):
    return lax.dot_general(rows, cols, (((1,), (1,)), ((), ())), precision=exact)


def butterfly_sum(x, axes):
    for axis in axes:
        count = lax.axis_size(axis)
        if count & (count - 1):
            x = lax.psum(x, axis)
            continue
        step = 1
        while step < count:
            x = x + lax.ppermute(x, axis, [(i, i ^ step) for i in range(count)])
            step *= 2
    return x


def local(residual, points, noise, block_list):
    field = residual[:, 0]
    coords = points[:, 0]
    nugget = noise[0]
    own_rows = field.shape[1]
    own_blocks = own_rows // BS
    first_block = lax.axis_index("blk") * own_blocks
    listed = block_list[0].astype(jnp.float32)
    nine = jnp.concatenate(
        [listed[:REACH], jnp.ones((1, listed.shape[1]), jnp.float32), listed[REACH:]], axis=0
    )
    margin = S * REACH
    wrapped = jnp.concatenate([nine[:, -margin:], nine, nine[:, :margin]], axis=1)
    powers = [field]
    rim = REACH * BS
    coords_wide = extended(coords, (("blk", 1),), rim)
    own_weights = lax.dynamic_slice_in_dim(wrapped, first_block + margin, own_blocks, 1)
    tiles = lax.optimization_barrier(band_tiles(coords_wide, own_weights, own_blocks))
    current = field
    for power_step in range(S):
        widened = extended(current, (("blk", 1),), rim)
        current = (
            band_product(widened, tiles, own_blocks)
            + (nugget - centre_shift) * current
        )
        powers.append(current)
    half_panel = jnp.stack(powers, axis=0)
    count_points = own_rows * lax.axis_size("blk") * lax.axis_size("leaf")
    sides_here = field.shape[0]
    whole = lax.all_gather(half_panel, "rhs", axis=1, tiled=True)
    flat = whole.reshape(-1, own_rows)
    gram = butterfly_sum(row_products(flat[: S * M], flat), ("leaf", "blk"))
    inverse_low, combo = galerkin(gram, count_points, M)
    first_rows = flat[: S * M]
    image = flat[M:] + centre_shift * first_rows
    part = lax.axis_index("rhs")
    basis_here = S * M // lax.axis_size("rhs")
    mine_low = lax.dynamic_slice_in_dim(inverse_low, part * basis_here, basis_here, 0)
    mine_combo = lax.dynamic_slice_in_dim(combo, part * sides_here, sides_here, 0)
    correction = jnp.dot(mine_combo, first_rows, precision=exact)
    new_residual = field - jnp.dot(mine_combo, image, precision=exact)
    basis = jnp.dot(mine_low, first_rows, precision=exact)
    return (correction[:, None], new_residual[:, None], basis[:, None])


def solution(mesh):
    placed = (
        P("rhs", "leaf", "blk"),
        P(None, "leaf", "blk"),
        P("leaf", "blk"),
        P("leaf", None, None),
    )
    return jax.shard_map(
        local,
        mesh=mesh,
        in_specs=placed,
        out_specs=(P("rhs", "leaf", "blk"), P("rhs", "leaf", "blk"), P("rhs", "leaf", "blk")),
        check_vma=False,
    )
```

```python
import jax
import jax.numpy as jnp
from jax import lax
from jax.sharding import PartitionSpec as P

M = 32
S = 4
BS = 256
REACH = 4
SUPPORT = 1408


centre_shift = 1.5
amplitude = 1.1
exact = lax.Precision.HIGHEST


def extended(x, axes, count, width):
    length = x.shape[1]
    up = [(i, (i + 1) % count) for i in range(count)]
    down = [(j, i) for i, j in up]
    before = lax.ppermute(x[:, length - width :], axes, up)
    after = lax.ppermute(x[:, :width], axes, down)
    return jnp.concatenate([before, x, after], axis=1)


def swap_pair(x, part):
    return lax.ppermute(x, "rhs", [(0, 1), (1, 0)])


def in_order(mine, other, part, axis):
    first = jnp.concatenate([mine, other], axis=axis)
    second = jnp.concatenate([other, mine], axis=axis)
    return jnp.where(part == 0, first, second)


def kernel_tile(near_points, own_points):
    squared = (near_points[0][:, None] - own_points[0][None, :]) ** 2
    squared = squared + (near_points[1][:, None] - own_points[1][None, :]) ** 2
    squared = squared + (near_points[2][:, None] - own_points[2][None, :]) ** 2
    radius = jnp.sqrt(squared) / SUPPORT
    remain = jnp.maximum(1.0 - radius, 0.0)
    return remain * remain * (remain * remain) * (4.0 * radius + 1.0) * (amplitude / SUPPORT)


def band_tiles(points_wide, weights, rows_out):
    width = 2 * REACH + 1
    blocks = points_wide.reshape(3, -1, BS)
    own = blocks[:, REACH : REACH + rows_out]
    near = jnp.stack([blocks[:, k : k + rows_out] for k in range(width)], axis=2)
    tiles = jax.vmap(jax.vmap(kernel_tile, in_axes=(1, None)), in_axes=(1, 1))(near, own)
    return tiles * jnp.transpose(weights)[:, :, None, None]


def band_product(field_wide, tiles, rows_out):
    width = 2 * REACH + 1
    count = field_wide.shape[0]
    blocks = field_wide.reshape(count, -1, BS)
    near = jnp.stack([blocks[:, k : k + rows_out] for k in range(width)], axis=2)
    out = jnp.einsum("mbkq,bkqp->mbp", near, tiles, precision=exact)
    return out.reshape(count, rows_out * BS)


def galerkin(gram, count_points, count_sides):
    normed = gram / count_points
    basis_count = normed.shape[0]
    gram_basis = normed[:basis_count, :basis_count]
    factor_low = jnp.linalg.cholesky(gram_basis)
    inverse_low = lax.linalg.triangular_solve(
        factor_low, jnp.eye(basis_count, dtype=jnp.float32), left_side=True, lower=True
    )
    cross = normed[:basis_count, count_sides:] + centre_shift * gram_basis
    projected = jnp.dot(
        jnp.dot(inverse_low, cross, precision=exact), inverse_low.T, precision=exact
    )
    projected = 0.5 * (projected + projected.T)
    small_side = jnp.dot(inverse_low, gram_basis[:, :count_sides], precision=exact)
    proj_factor = jnp.linalg.cholesky(projected)
    halfway = lax.linalg.triangular_solve(proj_factor, small_side, left_side=True, lower=True)
    coeffs = lax.linalg.triangular_solve(
        proj_factor, halfway, left_side=True, lower=True, transpose_a=True
    )
    combo = jnp.dot(coeffs.T, inverse_low, precision=exact)
    return (inverse_low, combo)


def row_products(rows, cols):
    return lax.dot_general(rows, cols, (((1,), (1,)), ((), ())), precision=exact)


def butterfly_sum(x, axes):
    for axis in axes:
        count = lax.axis_size(axis)
        if count & (count - 1):
            x = lax.psum(x, axis)
            continue
        step = 1
        while step < count:
            x = x + lax.ppermute(x, axis, [(i, i ^ step) for i in range(count)])
            step *= 2
    return x


def local(residual, points, noise, block_list):
    part = lax.axis_index("rhs")
    pairs = lax.axis_size("rhs")
    whole_field = residual[:, 0]
    half = whole_field.shape[1] // pairs
    mine = lax.dynamic_slice_in_dim(whole_field, part * half, half, 1)
    sent = lax.dynamic_slice_in_dim(whole_field, (1 - part) * half, half, 1)
    field = in_order(mine, swap_pair(sent, part), part, 0)
    coords = lax.dynamic_slice_in_dim(points[:, 0], part * half, half, 1)
    nugget = lax.dynamic_slice_in_dim(noise[0], part * half, half, 0)
    own_blocks = half // BS
    ring = lax.axis_size("blk") * pairs
    first_block = (lax.axis_index("blk") * pairs + part) * own_blocks
    listed = block_list[0].astype(jnp.float32)
    nine = jnp.concatenate(
        [listed[:REACH], jnp.ones((1, listed.shape[1]), jnp.float32), listed[REACH:]], axis=0
    )
    margin = S * REACH
    wrapped = jnp.concatenate([nine[:, -margin:], nine, nine[:, :margin]], axis=1)
    powers = [field]
    rim = REACH * BS
    coords_wide = extended(coords, ("blk", "rhs"), ring, rim)
    own_weights = lax.dynamic_slice_in_dim(wrapped, first_block + margin, own_blocks, 1)
    tiles = lax.optimization_barrier(band_tiles(coords_wide, own_weights, own_blocks))
    current = field
    for power_step in range(S):
        widened = extended(current, ("blk", "rhs"), ring, rim)
        current = band_product(widened, tiles, own_blocks) + (nugget - centre_shift) * current
        powers.append(current)
    flat = jnp.concatenate(powers, axis=0)
    count_points = half * ring * lax.axis_size("leaf")
    gram = butterfly_sum(row_products(flat[: S * M], flat), ("leaf", "blk", "rhs"))
    inverse_low, combo = galerkin(gram, count_points, M)
    first_rows = flat[: S * M]
    image = flat[M:] + centre_shift * first_rows
    correction = jnp.dot(combo, first_rows, precision=exact)
    new_residual = field - jnp.dot(combo, image, precision=exact)
    basis = jnp.dot(inverse_low, first_rows, precision=exact)
    results = []
    for full in (correction, new_residual, basis):
        groups = full.reshape(pairs, -1, half)
        keep = lax.dynamic_index_in_dim(groups, part, 0, False)
        give = lax.dynamic_index_in_dim(groups, 1 - part, 0, False)
        results.append(in_order(keep, swap_pair(give, part), part, 1)[:, None])
    return tuple(results)


def solution(mesh):
    placed = (
        P("rhs", "leaf", "blk"),
        P(None, "leaf", "blk"),
        P("leaf", "blk"),
        P("leaf", None, None),
    )
    return jax.shard_map(
        local,
        mesh=mesh,
        in_specs=placed,
        out_specs=(P("rhs", "leaf", "blk"), P("rhs", "leaf", "blk"), P("rhs", "leaf", "blk")),
        check_vma=False,
    )
```

```python
import jax
import jax.numpy as jnp
from jax import lax
from jax.sharding import PartitionSpec as P

M = 32
S = 4
BS = 256
REACH = 4
SUPPORT = 1408


centre_shift = 1.5
amplitude = 1.1
exact = lax.Precision.HIGHEST


def extended(x, axes, count, width):
    length = x.shape[1]
    up = [(i, (i + 1) % count) for i in range(count)]
    down = [(j, i) for i, j in up]
    before = lax.ppermute(x[:, length - width :], axes, up)
    after = lax.ppermute(x[:, :width], axes, down)
    return jnp.concatenate([before, x, after], axis=1)


def swap_pair(x, part):
    return lax.ppermute(x, "rhs", [(0, 1), (1, 0)])


def in_order(mine, other, part, axis):
    first = jnp.concatenate([mine, other], axis=axis)
    second = jnp.concatenate([other, mine], axis=axis)
    return jnp.where(part == 0, first, second)


def kernel_tile(near_points, own_points):
    squared = (near_points[0][:, None] - own_points[0][None, :]) ** 2
    squared = squared + (near_points[1][:, None] - own_points[1][None, :]) ** 2
    squared = squared + (near_points[2][:, None] - own_points[2][None, :]) ** 2
    radius = jnp.sqrt(squared) / SUPPORT
    remain = jnp.maximum(1.0 - radius, 0.0)
    return remain * remain * (remain * remain) * (4.0 * radius + 1.0) * (amplitude / SUPPORT)


def band_tiles(points_wide, weights, rows_out):
    width = 2 * REACH + 1
    blocks = points_wide.reshape(3, -1, BS)
    own = blocks[:, REACH : REACH + rows_out]
    near = jnp.stack([blocks[:, k : k + rows_out] for k in range(width)], axis=2)
    tiles = jax.vmap(jax.vmap(kernel_tile, in_axes=(1, None)), in_axes=(1, 1))(near, own)
    return tiles * jnp.transpose(weights)[:, :, None, None]


def band_product(field_wide, tiles, rows_out):
    width = 2 * REACH + 1
    count = field_wide.shape[0]
    blocks = field_wide.reshape(count, -1, BS)
    near = jnp.stack([blocks[:, k : k + rows_out] for k in range(width)], axis=2)
    out = jnp.einsum("mbkq,bkqp->mbp", near, tiles, precision=exact)
    return out.reshape(count, rows_out * BS)


def galerkin(gram, count_points, count_sides):
    normed = gram / count_points
    basis_count = normed.shape[0]
    gram_basis = normed[:basis_count, :basis_count]
    factor_low = jnp.linalg.cholesky(gram_basis)
    inverse_low = lax.linalg.triangular_solve(
        factor_low, jnp.eye(basis_count, dtype=jnp.float32), left_side=True, lower=True
    )
    cross = normed[:basis_count, count_sides:] + centre_shift * gram_basis
    projected = jnp.dot(
        jnp.dot(inverse_low, cross, precision=exact), inverse_low.T, precision=exact
    )
    projected = 0.5 * (projected + projected.T)
    small_side = jnp.dot(inverse_low, gram_basis[:, :count_sides], precision=exact)
    proj_factor = jnp.linalg.cholesky(projected)
    halfway = lax.linalg.triangular_solve(proj_factor, small_side, left_side=True, lower=True)
    coeffs = lax.linalg.triangular_solve(
        proj_factor, halfway, left_side=True, lower=True, transpose_a=True
    )
    combo = jnp.dot(coeffs.T, inverse_low, precision=exact)
    return (inverse_low, combo)


def row_products(rows, cols):
    return lax.dot_general(rows, cols, (((1,), (1,)), ((), ())), precision=exact)


def butterfly_sum(x, axes):
    count = 1
    for axis in axes:
        count *= lax.axis_size(axis)
    if count & (count - 1):
        return lax.psum(x, axes)

    def swap(value, mask):
        return lax.ppermute(value, axes, [(i, i ^ mask) for i in range(count)])

    step = 1
    while step * 4 <= count:
        near = x + swap(x, step)
        far = swap(x, 2 * step) + swap(x, 3 * step)
        x = near + far
        step *= 4
    if step < count:
        x = x + swap(x, step)
    return x


def local(residual, points, noise, block_list):
    part = lax.axis_index("rhs")
    pairs = lax.axis_size("rhs")
    whole_field = residual[:, 0]
    half = whole_field.shape[1] // pairs
    mine = lax.dynamic_slice_in_dim(whole_field, part * half, half, 1)
    sent = lax.dynamic_slice_in_dim(whole_field, (1 - part) * half, half, 1)
    field = in_order(mine, swap_pair(sent, part), part, 0)
    coords = lax.dynamic_slice_in_dim(points[:, 0], part * half, half, 1)
    nugget = lax.dynamic_slice_in_dim(noise[0], part * half, half, 0)
    own_blocks = half // BS
    ring = lax.axis_size("blk") * pairs
    first_block = (lax.axis_index("blk") * pairs + part) * own_blocks
    listed = block_list[0].astype(jnp.float32)
    nine = jnp.concatenate(
        [listed[:REACH], jnp.ones((1, listed.shape[1]), jnp.float32), listed[REACH:]], axis=0
    )
    margin = S * REACH
    wrapped = jnp.concatenate([nine[:, -margin:], nine, nine[:, :margin]], axis=1)
    powers = [field]
    rim = REACH * BS
    coords_wide = extended(coords, ("blk", "rhs"), ring, rim)
    own_weights = lax.dynamic_slice_in_dim(wrapped, first_block + margin, own_blocks, 1)
    tiles = lax.optimization_barrier(band_tiles(coords_wide, own_weights, own_blocks))
    current = field
    for power_step in range(S):
        widened = extended(current, ("blk", "rhs"), ring, rim)
        current = band_product(widened, tiles, own_blocks) + (nugget - centre_shift) * current
        powers.append(current)
    flat = jnp.concatenate(powers, axis=0)
    count_points = half * ring * lax.axis_size("leaf")
    gram = butterfly_sum(row_products(flat[: S * M], flat), ("blk", "leaf", "rhs"))
    inverse_low, combo = galerkin(gram, count_points, M)
    first_rows = flat[: S * M]
    image = flat[M:] + centre_shift * first_rows
    correction = jnp.dot(combo, first_rows, precision=exact)
    new_residual = field - jnp.dot(combo, image, precision=exact)
    basis = jnp.dot(inverse_low, first_rows, precision=exact)
    results = []
    for full in (correction, new_residual, basis):
        groups = full.reshape(pairs, -1, half)
        keep = lax.dynamic_index_in_dim(groups, part, 0, False)
        give = lax.dynamic_index_in_dim(groups, 1 - part, 0, False)
        results.append(in_order(keep, swap_pair(give, part), part, 1)[:, None])
    return tuple(results)


def solution(mesh):
    placed = (
        P("rhs", "leaf", "blk"),
        P(None, "leaf", "blk"),
        P("leaf", "blk"),
        P("leaf", None, None),
    )
    return jax.shard_map(
        local,
        mesh=mesh,
        in_specs=placed,
        out_specs=(P("rhs", "leaf", "blk"), P("rhs", "leaf", "blk"), P("rhs", "leaf", "blk")),
        check_vma=False,
    )
```

```python
import functools
import jax
import jax.numpy as jnp
from jax import lax
from jax.sharding import PartitionSpec as P
from jax.experimental import pallas as pl
from jax.experimental.pallas import tpu as pltpu

M = 32
S = 4
BS = 256
REACH = 4
SUPPORT = 1408


centre_shift = 1.5
amplitude = 1.1
exact = lax.Precision.HIGHEST


def extended(x, axes, count, width):
    length = x.shape[1]
    up = [(i, (i + 1) % count) for i in range(count)]
    down = [(j, i) for i, j in up]
    before = lax.ppermute(x[:, length - width :], axes, up)
    after = lax.ppermute(x[:, :width], axes, down)
    return jnp.concatenate([before, x, after], axis=1)


def halo_kernel(pairs, ring, width, x_ref, out_ref, edges, send_sem, recv_sem):
    length = x_ref.shape[1]
    leaf = lax.axis_index("leaf")
    me = lax.axis_index("blk") * pairs + lax.axis_index("rhs")
    up = lax.rem(me + 1, ring)
    down = lax.rem(me + ring - 1, ring)
    up_id = (up // pairs, leaf, up % pairs)
    down_id = (down // pairs, leaf, down % pairs)
    barrier = pltpu.get_barrier_semaphore()
    for target in (up_id, down_id):
        pl.semaphore_signal(barrier, inc=1, device_id=target, device_id_type=pl.DeviceIdType.MESH)
    pl.semaphore_wait(barrier, 2)
    to_up = pltpu.make_async_remote_copy(
        src_ref=x_ref.at[:, pl.ds(length - width, width)],
        dst_ref=edges.at[0],
        send_sem=send_sem.at[0],
        recv_sem=recv_sem.at[0],
        device_id=up_id,
        device_id_type=pl.DeviceIdType.MESH,
    )
    to_down = pltpu.make_async_remote_copy(
        src_ref=x_ref.at[:, pl.ds(0, width)],
        dst_ref=edges.at[1],
        send_sem=send_sem.at[1],
        recv_sem=recv_sem.at[1],
        device_id=down_id,
        device_id_type=pl.DeviceIdType.MESH,
    )
    to_up.start()
    to_down.start()
    out_ref[:, pl.ds(width, length)] = x_ref[...]
    to_up.wait()
    to_down.wait()
    out_ref[:, pl.ds(0, width)] = edges[0]
    out_ref[:, pl.ds(width + length, width)] = edges[1]


def halo_exchange(x, width, tag):
    pairs = lax.axis_size("rhs")
    ring = lax.axis_size("blk") * pairs
    rows, length = x.shape
    return pl.pallas_call(
        functools.partial(halo_kernel, pairs, ring, width),
        out_shape=jax.ShapeDtypeStruct((rows, length + 2 * width), x.dtype),
        in_specs=[pl.BlockSpec(memory_space=pltpu.VMEM)],
        out_specs=pl.BlockSpec(memory_space=pltpu.VMEM),
        scratch_shapes=[
            pltpu.VMEM((2, rows, width), x.dtype),
            pltpu.SemaphoreType.DMA((2,)),
            pltpu.SemaphoreType.DMA((2,)),
        ],
        compiler_params=pltpu.CompilerParams(collective_id=tag, has_side_effects=True),
    )(x)


def swap_pair(x, part):
    return lax.ppermute(x, "rhs", [(0, 1), (1, 0)])


def in_order(mine, other, part, axis):
    first = jnp.concatenate([mine, other], axis=axis)
    second = jnp.concatenate([other, mine], axis=axis)
    return jnp.where(part == 0, first, second)


def kernel_tile(near_points, own_points):
    squared = (near_points[0][:, None] - own_points[0][None, :]) ** 2
    squared = squared + (near_points[1][:, None] - own_points[1][None, :]) ** 2
    squared = squared + (near_points[2][:, None] - own_points[2][None, :]) ** 2
    radius = jnp.sqrt(squared) / SUPPORT
    remain = jnp.maximum(1.0 - radius, 0.0)
    return remain * remain * (remain * remain) * (4.0 * radius + 1.0) * (amplitude / SUPPORT)


def band_tiles(points_wide, weights, rows_out):
    width = 2 * REACH + 1
    blocks = points_wide.reshape(3, -1, BS)
    own = blocks[:, REACH : REACH + rows_out]
    near = jnp.stack([blocks[:, k : k + rows_out] for k in range(width)], axis=2)
    tiles = jax.vmap(jax.vmap(kernel_tile, in_axes=(1, None)), in_axes=(1, 1))(near, own)
    return tiles * jnp.transpose(weights)[:, :, None, None]


def band_product(field_wide, tiles, rows_out):
    width = 2 * REACH + 1
    count = field_wide.shape[0]
    blocks = field_wide.reshape(count, -1, BS)
    near = jnp.stack([blocks[:, k : k + rows_out] for k in range(width)], axis=2)
    out = jnp.einsum("mbkq,bkqp->mbp", near, tiles, precision=exact)
    return out.reshape(count, rows_out * BS)


def galerkin(gram, count_points, count_sides):
    normed = gram / count_points
    basis_count = normed.shape[0]
    gram_basis = normed[:basis_count, :basis_count]
    factor_low = jnp.linalg.cholesky(gram_basis)
    inverse_low = lax.linalg.triangular_solve(
        factor_low, jnp.eye(basis_count, dtype=jnp.float32), left_side=True, lower=True
    )
    cross = normed[:basis_count, count_sides:] + centre_shift * gram_basis
    projected = jnp.dot(
        jnp.dot(inverse_low, cross, precision=exact), inverse_low.T, precision=exact
    )
    projected = 0.5 * (projected + projected.T)
    small_side = jnp.dot(inverse_low, gram_basis[:, :count_sides], precision=exact)
    proj_factor = jnp.linalg.cholesky(projected)
    halfway = lax.linalg.triangular_solve(proj_factor, small_side, left_side=True, lower=True)
    coeffs = lax.linalg.triangular_solve(
        proj_factor, halfway, left_side=True, lower=True, transpose_a=True
    )
    combo = jnp.dot(coeffs.T, inverse_low, precision=exact)
    return (inverse_low, combo)


def row_products(rows, cols):
    return lax.dot_general(rows, cols, (((1,), (1,)), ((), ())), precision=exact)


def butterfly_sum(x, axes):
    for axis in axes:
        count = lax.axis_size(axis)
        if count & (count - 1):
            x = lax.psum(x, axis)
            continue
        step = 1
        while step < count:
            x = x + lax.ppermute(x, axis, [(i, i ^ step) for i in range(count)])
            step *= 2
    return x


def local(residual, points, noise, block_list):
    part = lax.axis_index("rhs")
    pairs = lax.axis_size("rhs")
    whole_field = residual[:, 0]
    half = whole_field.shape[1] // pairs
    mine = lax.dynamic_slice_in_dim(whole_field, part * half, half, 1)
    sent = lax.dynamic_slice_in_dim(whole_field, (1 - part) * half, half, 1)
    field = in_order(mine, swap_pair(sent, part), part, 0)
    coords = lax.dynamic_slice_in_dim(points[:, 0], part * half, half, 1)
    nugget = lax.dynamic_slice_in_dim(noise[0], part * half, half, 0)
    own_blocks = half // BS
    ring = lax.axis_size("blk") * pairs
    first_block = (lax.axis_index("blk") * pairs + part) * own_blocks
    listed = block_list[0].astype(jnp.float32)
    nine = jnp.concatenate(
        [listed[:REACH], jnp.ones((1, listed.shape[1]), jnp.float32), listed[REACH:]], axis=0
    )
    margin = S * REACH
    wrapped = jnp.concatenate([nine[:, -margin:], nine, nine[:, :margin]], axis=1)
    powers = [field]
    rim = REACH * BS
    coords_wide = halo_exchange(coords, rim, 0)
    own_weights = lax.dynamic_slice_in_dim(wrapped, first_block + margin, own_blocks, 1)
    tiles = lax.optimization_barrier(band_tiles(coords_wide, own_weights, own_blocks))
    current = field
    for power_step in range(S):
        widened = halo_exchange(current, rim, 1)
        current = band_product(widened, tiles, own_blocks) + (nugget - centre_shift) * current
        powers.append(current)
    flat = jnp.concatenate(powers, axis=0)
    count_points = half * ring * lax.axis_size("leaf")
    gram = butterfly_sum(row_products(flat[: S * M], flat), ("leaf", "blk", "rhs"))
    inverse_low, combo = galerkin(gram, count_points, M)
    first_rows = flat[: S * M]
    image = flat[M:] + centre_shift * first_rows
    correction = jnp.dot(combo, first_rows, precision=exact)
    new_residual = field - jnp.dot(combo, image, precision=exact)
    basis = jnp.dot(inverse_low, first_rows, precision=exact)
    results = []
    for full in (correction, new_residual, basis):
        groups = full.reshape(pairs, -1, half)
        keep = lax.dynamic_index_in_dim(groups, part, 0, False)
        give = lax.dynamic_index_in_dim(groups, 1 - part, 0, False)
        results.append(in_order(keep, swap_pair(give, part), part, 1)[:, None])
    return tuple(results)


def solution(mesh):
    placed = (
        P("rhs", "leaf", "blk"),
        P(None, "leaf", "blk"),
        P("leaf", "blk"),
        P("leaf", None, None),
    )
    return jax.shard_map(
        local,
        mesh=mesh,
        in_specs=placed,
        out_specs=(P("rhs", "leaf", "blk"), P("rhs", "leaf", "blk"), P("rhs", "leaf", "blk")),
        check_vma=False,
    )
```

```python
import jax
import jax.numpy as jnp
from jax import lax
from jax.sharding import PartitionSpec as P

M = 32
S = 4
BS = 256
REACH = 4
SUPPORT = 1408


centre_shift = 1.5
amplitude = 1.1
exact = lax.Precision.HIGHEST


def extended(x, axes, count, width):
    length = x.shape[1]
    up = [(i, (i + 1) % count) for i in range(count)]
    down = [(j, i) for i, j in up]
    before = lax.ppermute(x[:, length - width :], axes, up)
    after = lax.ppermute(x[:, :width], axes, down)
    return jnp.concatenate([before, x, after], axis=1)


def swap_pair(x, part):
    return lax.ppermute(x, "rhs", [(0, 1), (1, 0)])


def in_order(mine, other, part, axis):
    first = jnp.concatenate([mine, other], axis=axis)
    second = jnp.concatenate([other, mine], axis=axis)
    return jnp.where(part == 0, first, second)


def kernel_tile(near_points, own_points):
    squared = (near_points[0][:, None] - own_points[0][None, :]) ** 2
    squared = squared + (near_points[1][:, None] - own_points[1][None, :]) ** 2
    squared = squared + (near_points[2][:, None] - own_points[2][None, :]) ** 2
    radius = jnp.sqrt(squared) / SUPPORT
    remain = jnp.maximum(1.0 - radius, 0.0)
    return remain * remain * (remain * remain) * (4.0 * radius + 1.0) * (amplitude / SUPPORT)


def band_tiles(points_wide, weights, rows_out):
    width = 2 * REACH + 1
    blocks = points_wide.reshape(3, -1, BS)
    own = blocks[:, REACH : REACH + rows_out]
    near = jnp.stack([blocks[:, k : k + rows_out] for k in range(width)], axis=2)
    tiles = jax.vmap(jax.vmap(kernel_tile, in_axes=(1, None)), in_axes=(1, 1))(near, own)
    return tiles * jnp.transpose(weights)[:, :, None, None]


def band_product(field_wide, tiles, rows_out):
    width = 2 * REACH + 1
    count = field_wide.shape[0]
    blocks = field_wide.reshape(count, -1, BS)
    near = jnp.stack([blocks[:, k : k + rows_out] for k in range(width)], axis=2)
    out = jnp.einsum("mbkq,bkqp->mbp", near, tiles, precision=exact)
    return out.reshape(count, rows_out * BS)


def galerkin(gram, count_points, count_sides):
    normed = gram / count_points
    basis_count = normed.shape[0]
    gram_basis = normed[:basis_count, :basis_count]
    factor_low = jnp.linalg.cholesky(gram_basis)
    inverse_low = lax.linalg.triangular_solve(
        factor_low, jnp.eye(basis_count, dtype=jnp.float32), left_side=True, lower=True
    )
    cross = normed[:basis_count, count_sides:] + centre_shift * gram_basis
    projected = jnp.dot(
        jnp.dot(inverse_low, cross, precision=exact), inverse_low.T, precision=exact
    )
    projected = 0.5 * (projected + projected.T)
    small_side = jnp.dot(inverse_low, gram_basis[:, :count_sides], precision=exact)
    proj_factor = jnp.linalg.cholesky(projected)
    halfway = lax.linalg.triangular_solve(proj_factor, small_side, left_side=True, lower=True)
    coeffs = lax.linalg.triangular_solve(
        proj_factor, halfway, left_side=True, lower=True, transpose_a=True
    )
    combo = jnp.dot(coeffs.T, inverse_low, precision=exact)
    return (inverse_low, combo)


def row_products(rows, cols):
    return lax.dot_general(rows, cols, (((1,), (1,)), ((), ())), precision=exact)


def butterfly_sum(x, axes):
    for axis in axes:
        count = lax.axis_size(axis)
        if count & (count - 1):
            x = lax.psum(x, axis)
            continue
        step = 1
        while step < count:
            x = x + lax.ppermute(x, axis, [(i, i ^ step) for i in range(count)])
            step *= 2
    return x


def local(residual, points, noise, block_list):
    part = lax.axis_index("rhs")
    pairs = lax.axis_size("rhs")
    whole_field = residual[:, 0]
    half = whole_field.shape[1] // pairs
    mine = lax.dynamic_slice_in_dim(whole_field, part * half, half, 1)
    sent = lax.dynamic_slice_in_dim(whole_field, (1 - part) * half, half, 1)
    field = in_order(mine, swap_pair(sent, part), part, 0)
    coords = lax.dynamic_slice_in_dim(points[:, 0], part * half, half, 1)
    nugget = lax.dynamic_slice_in_dim(noise[0], part * half, half, 0)
    own_blocks = half // BS
    ring = lax.axis_size("blk") * pairs
    first_block = (lax.axis_index("blk") * pairs + part) * own_blocks
    listed = block_list[0].astype(jnp.float32)
    nine = jnp.concatenate(
        [listed[:REACH], jnp.ones((1, listed.shape[1]), jnp.float32), listed[REACH:]], axis=0
    )
    margin = S * REACH
    wrapped = jnp.concatenate([nine[:, -margin:], nine, nine[:, :margin]], axis=1)
    powers = [field]
    rim = REACH * BS
    coords_wide = extended(coords, ("blk", "rhs"), ring, rim)
    own_weights = lax.dynamic_slice_in_dim(wrapped, first_block + margin, own_blocks, 1)
    tiles = lax.optimization_barrier(band_tiles(coords_wide, own_weights, own_blocks))
    current = field
    for power_step in range(S):
        widened = extended(current, ("blk", "rhs"), ring, rim)
        current = band_product(widened, tiles, own_blocks) + (nugget - centre_shift) * current
        powers.append(current)
    flat = jnp.concatenate(powers, axis=0)
    count_points = half * ring * lax.axis_size("leaf")
    gram = butterfly_sum(row_products(flat[: S * M], flat), ("leaf", "blk", "rhs"))
    inverse_low, combo = galerkin(gram, count_points, M)
    first_rows = flat[: S * M]
    image = flat[M:] + centre_shift * first_rows
    sides = M // pairs
    basis_rows = S * M // pairs

    def rows_for(group):
        mix = lax.dynamic_slice_in_dim(combo, group * sides, sides, 0)
        low = lax.dynamic_slice_in_dim(inverse_low, group * basis_rows, basis_rows, 0)
        start = lax.dynamic_slice_in_dim(field, group * sides, sides, 0)
        correction = jnp.dot(mix, first_rows, precision=exact)
        new_residual = start - jnp.dot(mix, image, precision=exact)
        basis = jnp.dot(low, first_rows, precision=exact)
        return jnp.concatenate([correction, new_residual, basis], axis=0)

    got = swap_pair(rows_for(1 - part), part)
    kept = rows_for(part)
    joined = in_order(kept, got, part, 1)
    results = [
        joined[:sides, None],
        joined[sides : 2 * sides, None],
        joined[2 * sides :, None],
    ]
    return tuple(results)


def solution(mesh):
    placed = (
        P("rhs", "leaf", "blk"),
        P(None, "leaf", "blk"),
        P("leaf", "blk"),
        P("leaf", None, None),
    )
    return jax.shard_map(
        local,
        mesh=mesh,
        in_specs=placed,
        out_specs=(P("rhs", "leaf", "blk"), P("rhs", "leaf", "blk"), P("rhs", "leaf", "blk")),
        check_vma=False,
    )
```

```python
import jax
import jax.numpy as jnp
from jax import lax
from jax.sharding import PartitionSpec as P

M = 32
S = 4
BS = 256
REACH = 4
SUPPORT = 1408


centre_shift = 1.5
amplitude = 1.1
exact = lax.Precision.HIGHEST


def extended(x, axes, count, width):
    length = x.shape[1]
    up = [(i, (i + 1) % count) for i in range(count)]
    down = [(j, i) for i, j in up]
    before = lax.ppermute(x[:, length - width :], axes, up)
    after = lax.ppermute(x[:, :width], axes, down)
    return jnp.concatenate([before, x, after], axis=1)


def swap_pair(x, part):
    return lax.ppermute(x, "rhs", [(0, 1), (1, 0)])


def in_order(mine, other, part, axis):
    first = jnp.concatenate([mine, other], axis=axis)
    second = jnp.concatenate([other, mine], axis=axis)
    return jnp.where(part == 0, first, second)


def kernel_tile(near_points, own_points):
    squared = (near_points[0][:, None] - own_points[0][None, :]) ** 2
    squared = squared + (near_points[1][:, None] - own_points[1][None, :]) ** 2
    squared = squared + (near_points[2][:, None] - own_points[2][None, :]) ** 2
    radius = jnp.sqrt(squared) / SUPPORT
    remain = jnp.maximum(1.0 - radius, 0.0)
    return remain * remain * (remain * remain) * (4.0 * radius + 1.0) * (amplitude / SUPPORT)


def band_tiles(points_wide, weights, rows_out):
    width = 2 * REACH + 1
    blocks = points_wide.reshape(3, -1, BS)
    own = blocks[:, REACH : REACH + rows_out]
    near = jnp.stack([blocks[:, k : k + rows_out] for k in range(width)], axis=2)
    tiles = jax.vmap(jax.vmap(kernel_tile, in_axes=(1, None)), in_axes=(1, 1))(near, own)
    return tiles * jnp.transpose(weights)[:, :, None, None]


def band_product(field_wide, tiles, rows_out):
    width = 2 * REACH + 1
    count = field_wide.shape[0]
    blocks = field_wide.reshape(count, -1, BS)
    near = jnp.stack([blocks[:, k : k + rows_out] for k in range(width)], axis=2)
    out = jnp.einsum("mbkq,bkqp->mbp", near, tiles, precision=exact)
    return out.reshape(count, rows_out * BS)


def galerkin(gram_basis_sum, gram_last_sum, count_points, count_sides):
    gram_basis = gram_basis_sum / count_points
    basis_count = gram_basis.shape[0]
    factor_low = jnp.linalg.cholesky(gram_basis)
    inverse_low = lax.linalg.triangular_solve(
        factor_low, jnp.eye(basis_count, dtype=jnp.float32), left_side=True, lower=True
    )
    normed_cross = jnp.concatenate(
        [gram_basis[:, count_sides:], gram_last_sum / count_points], axis=1
    )
    cross = normed_cross + centre_shift * gram_basis
    projected = jnp.dot(
        jnp.dot(inverse_low, cross, precision=exact), inverse_low.T, precision=exact
    )
    projected = 0.5 * (projected + projected.T)
    small_side = jnp.dot(inverse_low, gram_basis[:, :count_sides], precision=exact)
    proj_factor = jnp.linalg.cholesky(projected)
    halfway = lax.linalg.triangular_solve(proj_factor, small_side, left_side=True, lower=True)
    coeffs = lax.linalg.triangular_solve(
        proj_factor, halfway, left_side=True, lower=True, transpose_a=True
    )
    combo = jnp.dot(coeffs.T, inverse_low, precision=exact)
    return (inverse_low, combo)


def row_products(rows, cols):
    return lax.dot_general(rows, cols, (((1,), (1,)), ((), ())), precision=exact)


def butterfly_sum(x, axes):
    for axis in axes:
        count = lax.axis_size(axis)
        if count & (count - 1):
            x = lax.psum(x, axis)
            continue
        step = 1
        while step < count:
            x = x + lax.ppermute(x, axis, [(i, i ^ step) for i in range(count)])
            step *= 2
    return x


def local(residual, points, noise, block_list):
    part = lax.axis_index("rhs")
    pairs = lax.axis_size("rhs")
    whole_field = residual[:, 0]
    half = whole_field.shape[1] // pairs
    mine = lax.dynamic_slice_in_dim(whole_field, part * half, half, 1)
    sent = lax.dynamic_slice_in_dim(whole_field, (1 - part) * half, half, 1)
    field = in_order(mine, swap_pair(sent, part), part, 0)
    coords = lax.dynamic_slice_in_dim(points[:, 0], part * half, half, 1)
    nugget = lax.dynamic_slice_in_dim(noise[0], part * half, half, 0)
    own_blocks = half // BS
    ring = lax.axis_size("blk") * pairs
    first_block = (lax.axis_index("blk") * pairs + part) * own_blocks
    listed = block_list[0].astype(jnp.float32)
    nine = jnp.concatenate(
        [listed[:REACH], jnp.ones((1, listed.shape[1]), jnp.float32), listed[REACH:]], axis=0
    )
    margin = S * REACH
    wrapped = jnp.concatenate([nine[:, -margin:], nine, nine[:, :margin]], axis=1)
    powers = [field]
    rim = REACH * BS
    coords_wide = extended(coords, ("blk", "rhs"), ring, rim)
    own_weights = lax.dynamic_slice_in_dim(wrapped, first_block + margin, own_blocks, 1)
    tiles = lax.optimization_barrier(band_tiles(coords_wide, own_weights, own_blocks))
    current = field
    axes = ("leaf", "blk", "rhs")
    for power_step in range(S):
        widened = extended(current, ("blk", "rhs"), ring, rim)
        if power_step == S - 1:
            basis_rows = jnp.concatenate(powers, axis=0)
            gram_basis_sum = butterfly_sum(row_products(basis_rows, basis_rows), axes)
        current = band_product(widened, tiles, own_blocks) + (nugget - centre_shift) * current
        powers.append(current)
    flat = jnp.concatenate(powers, axis=0)
    count_points = half * ring * lax.axis_size("leaf")
    gram_last_sum = butterfly_sum(row_products(basis_rows, current), axes)
    inverse_low, combo = galerkin(gram_basis_sum, gram_last_sum, count_points, M)
    first_rows = flat[: S * M]
    image = flat[M:] + centre_shift * first_rows
    correction = jnp.dot(combo, first_rows, precision=exact)
    new_residual = field - jnp.dot(combo, image, precision=exact)
    basis = jnp.dot(inverse_low, first_rows, precision=exact)
    results = []
    for full in (correction, new_residual, basis):
        groups = full.reshape(pairs, -1, half)
        keep = lax.dynamic_index_in_dim(groups, part, 0, False)
        give = lax.dynamic_index_in_dim(groups, 1 - part, 0, False)
        results.append(in_order(keep, swap_pair(give, part), part, 1)[:, None])
    return tuple(results)


def solution(mesh):
    placed = (
        P("rhs", "leaf", "blk"),
        P(None, "leaf", "blk"),
        P("leaf", "blk"),
        P("leaf", None, None),
    )
    return jax.shard_map(
        local,
        mesh=mesh,
        in_specs=placed,
        out_specs=(P("rhs", "leaf", "blk"), P("rhs", "leaf", "blk"), P("rhs", "leaf", "blk")),
        check_vma=False,
    )
```

```python
import jax
import jax.numpy as jnp
from jax import lax
from jax.sharding import PartitionSpec as P

M = 32
S = 4
BS = 256
REACH = 4
SUPPORT = 1408


centre_shift = 1.5
amplitude = 1.1
exact = lax.Precision.HIGHEST


def extended(x, axes, count, width):
    length = x.shape[1]
    up = [(i, (i + 1) % count) for i in range(count)]
    down = [(j, i) for i, j in up]
    before = lax.ppermute(x[:, length - width :], axes, up)
    after = lax.ppermute(x[:, :width], axes, down)
    return jnp.concatenate([before, x, after], axis=1)


def swap_pair(x, part):
    return lax.ppermute(x, "rhs", [(0, 1), (1, 0)])


def in_order(mine, other, part, axis):
    first = jnp.concatenate([mine, other], axis=axis)
    second = jnp.concatenate([other, mine], axis=axis)
    return jnp.where(part == 0, first, second)


def kernel_tile(near_points, own_points):
    squared = (near_points[0][:, None] - own_points[0][None, :]) ** 2
    squared = squared + (near_points[1][:, None] - own_points[1][None, :]) ** 2
    squared = squared + (near_points[2][:, None] - own_points[2][None, :]) ** 2
    radius = jnp.sqrt(squared) / SUPPORT
    remain = jnp.maximum(1.0 - radius, 0.0)
    return remain * remain * (remain * remain) * (4.0 * radius + 1.0) * (amplitude / SUPPORT)


def band_tiles(points_wide, weights, rows_out):
    width = 2 * REACH + 1
    blocks = points_wide.reshape(3, -1, BS)
    own = blocks[:, REACH : REACH + rows_out]
    near = jnp.stack([blocks[:, k : k + rows_out] for k in range(width)], axis=2)
    tiles = jax.vmap(jax.vmap(kernel_tile, in_axes=(1, None)), in_axes=(1, 1))(near, own)
    return tiles * jnp.transpose(weights)[:, :, None, None]


def band_product(field_wide, tiles, first, rows_out):
    width = 2 * REACH + 1
    count = field_wide.shape[0]
    blocks = field_wide.reshape(count, -1, BS)
    near = jnp.stack([blocks[:, first + k : first + k + rows_out] for k in range(width)], axis=2)
    out = jnp.einsum("mbkq,bkqp->mbp", near, tiles[first : first + rows_out], precision=exact)
    return out.reshape(count, rows_out * BS)


def galerkin(gram, count_points, count_sides):
    normed = gram / count_points
    basis_count = normed.shape[0]
    gram_basis = normed[:basis_count, :basis_count]
    factor_low = jnp.linalg.cholesky(gram_basis)
    inverse_low = lax.linalg.triangular_solve(
        factor_low, jnp.eye(basis_count, dtype=jnp.float32), left_side=True, lower=True
    )
    cross = normed[:basis_count, count_sides:] + centre_shift * gram_basis
    projected = jnp.dot(
        jnp.dot(inverse_low, cross, precision=exact), inverse_low.T, precision=exact
    )
    projected = 0.5 * (projected + projected.T)
    small_side = jnp.dot(inverse_low, gram_basis[:, :count_sides], precision=exact)
    proj_factor = jnp.linalg.cholesky(projected)
    halfway = lax.linalg.triangular_solve(proj_factor, small_side, left_side=True, lower=True)
    coeffs = lax.linalg.triangular_solve(
        proj_factor, halfway, left_side=True, lower=True, transpose_a=True
    )
    combo = jnp.dot(coeffs.T, inverse_low, precision=exact)
    return (inverse_low, combo)


def row_products(rows, cols):
    return lax.dot_general(rows, cols, (((1,), (1,)), ((), ())), precision=exact)


def butterfly_sum(x, axes):
    for axis in axes:
        count = lax.axis_size(axis)
        if count & (count - 1):
            x = lax.psum(x, axis)
            continue
        step = 1
        while step < count:
            x = x + lax.ppermute(x, axis, [(i, i ^ step) for i in range(count)])
            step *= 2
    return x


def local(residual, points, noise, block_list):
    part = lax.axis_index("rhs")
    pairs = lax.axis_size("rhs")
    whole_field = residual[:, 0]
    half = whole_field.shape[1] // pairs
    mine = lax.dynamic_slice_in_dim(whole_field, part * half, half, 1)
    sent = lax.dynamic_slice_in_dim(whole_field, (1 - part) * half, half, 1)
    field = in_order(mine, swap_pair(sent, part), part, 0)
    coords = lax.dynamic_slice_in_dim(points[:, 0], part * half, half, 1)
    nugget = lax.dynamic_slice_in_dim(noise[0], part * half, half, 0)
    own_blocks = half // BS
    ring = lax.axis_size("blk") * pairs
    first_block = (lax.axis_index("blk") * pairs + part) * own_blocks
    listed = block_list[0].astype(jnp.float32)
    nine = jnp.concatenate(
        [listed[:REACH], jnp.ones((1, listed.shape[1]), jnp.float32), listed[REACH:]], axis=0
    )
    margin = S * REACH
    wrapped = jnp.concatenate([nine[:, -margin:], nine, nine[:, :margin]], axis=1)
    powers = [field]
    rim = REACH * BS
    coords_wide = extended(coords, ("blk", "rhs"), ring, rim)
    own_weights = lax.dynamic_slice_in_dim(wrapped, first_block + margin, own_blocks, 1)
    tiles = lax.optimization_barrier(band_tiles(coords_wide, own_weights, own_blocks))
    current = field
    widened = extended(current, ("blk", "rhs"), ring, rim)
    up = [(i, (i + 1) % ring) for i in range(ring)]
    down = [(j, i) for i, j in up]
    shift = nugget - centre_shift
    for power_step in range(S):
        spans = [(0, REACH), (REACH, own_blocks - 2 * REACH), (own_blocks - REACH, REACH)]
        pieces = []
        for first, rows_out in spans:
            if rows_out == 0:
                continue
            points_here = slice(first * BS, (first + rows_out) * BS)
            piece = band_product(widened, tiles, first, rows_out)
            pieces.append(piece + shift[points_here] * current[:, points_here])
        current = jnp.concatenate(pieces, axis=1)
        powers.append(current)
        if power_step < S - 1:
            after = lax.ppermute(pieces[0], ("blk", "rhs"), down)
            before = lax.ppermute(pieces[-1], ("blk", "rhs"), up)
            widened = jnp.concatenate([before, current, after], axis=1)
    flat = jnp.concatenate(powers, axis=0)
    count_points = half * ring * lax.axis_size("leaf")
    gram = butterfly_sum(row_products(flat[: S * M], flat), ("leaf", "blk", "rhs"))
    inverse_low, combo = galerkin(gram, count_points, M)
    first_rows = flat[: S * M]
    image = flat[M:] + centre_shift * first_rows
    correction = jnp.dot(combo, first_rows, precision=exact)
    new_residual = field - jnp.dot(combo, image, precision=exact)
    basis = jnp.dot(inverse_low, first_rows, precision=exact)
    results = []
    for full in (correction, new_residual, basis):
        groups = full.reshape(pairs, -1, half)
        keep = lax.dynamic_index_in_dim(groups, part, 0, False)
        give = lax.dynamic_index_in_dim(groups, 1 - part, 0, False)
        results.append(in_order(keep, swap_pair(give, part), part, 1)[:, None])
    return tuple(results)


def solution(mesh):
    placed = (
        P("rhs", "leaf", "blk"),
        P(None, "leaf", "blk"),
        P("leaf", "blk"),
        P("leaf", None, None),
    )
    return jax.shard_map(
        local,
        mesh=mesh,
        in_specs=placed,
        out_specs=(P("rhs", "leaf", "blk"), P("rhs", "leaf", "blk"), P("rhs", "leaf", "blk")),
        check_vma=False,
    )
```

```python
import jax
import jax.numpy as jnp
from jax import lax
from jax.sharding import PartitionSpec as P

M = 32
S = 4
BS = 256
REACH = 4
SUPPORT = 1408


centre_shift = 1.5
amplitude = 1.1
exact = lax.Precision.HIGHEST


def extended(x, axes, count, width):
    length = x.shape[1]
    up = [(i, (i + 1) % count) for i in range(count)]
    down = [(j, i) for i, j in up]
    before = lax.ppermute(x[:, length - width :], axes, up)
    after = lax.ppermute(x[:, :width], axes, down)
    return jnp.concatenate([before, x, after], axis=1)


def swap_pair(x, part):
    return lax.ppermute(x, "rhs", [(0, 1), (1, 0)])


def in_order(mine, other, part, axis):
    first = jnp.concatenate([mine, other], axis=axis)
    second = jnp.concatenate([other, mine], axis=axis)
    return jnp.where(part == 0, first, second)


def kernel_tile(near_points, own_points):
    squared = (near_points[0][:, None] - own_points[0][None, :]) ** 2
    squared = squared + (near_points[1][:, None] - own_points[1][None, :]) ** 2
    squared = squared + (near_points[2][:, None] - own_points[2][None, :]) ** 2
    radius = jnp.sqrt(squared) / SUPPORT
    remain = jnp.maximum(1.0 - radius, 0.0)
    return remain * remain * (remain * remain) * (4.0 * radius + 1.0) * (amplitude / SUPPORT)


def band_tiles(points_wide, weights, rows_out):
    width = 2 * REACH + 1
    blocks = points_wide.reshape(3, -1, BS)
    own = blocks[:, REACH : REACH + rows_out]
    near = jnp.stack([blocks[:, k : k + rows_out] for k in range(width)], axis=2)
    tiles = jax.vmap(jax.vmap(kernel_tile, in_axes=(1, None)), in_axes=(1, 1))(near, own)
    return tiles * jnp.transpose(weights)[:, :, None, None]


def band_product(field_wide, tiles, rows_out):
    width = 2 * REACH + 1
    count = field_wide.shape[0]
    blocks = field_wide.reshape(count, -1, BS)
    near = jnp.stack([blocks[:, k : k + rows_out] for k in range(width)], axis=2)
    out = jnp.einsum("mbkq,bkqp->mbp", near, tiles, precision=exact)
    return out.reshape(count, rows_out * BS)


def galerkin(gram, count_points, count_sides):
    normed = gram / count_points
    basis_count = normed.shape[0]
    gram_basis = normed[:basis_count, :basis_count]
    factor_low = jnp.linalg.cholesky(gram_basis)
    inverse_low = lax.linalg.triangular_solve(
        factor_low, jnp.eye(basis_count, dtype=jnp.float32), left_side=True, lower=True
    )
    cross = normed[:basis_count, count_sides:] + centre_shift * gram_basis
    projected = jnp.dot(
        jnp.dot(inverse_low, cross, precision=exact), inverse_low.T, precision=exact
    )
    projected = 0.5 * (projected + projected.T)
    small_side = jnp.dot(inverse_low, gram_basis[:, :count_sides], precision=exact)
    proj_factor = jnp.linalg.cholesky(projected)
    halfway = lax.linalg.triangular_solve(proj_factor, small_side, left_side=True, lower=True)
    coeffs = lax.linalg.triangular_solve(
        proj_factor, halfway, left_side=True, lower=True, transpose_a=True
    )
    combo = jnp.dot(coeffs.T, inverse_low, precision=exact)
    return (inverse_low, combo)


def row_products(rows, cols):
    return lax.dot_general(rows, cols, (((1,), (1,)), ((), ())), precision=exact)


def butterfly_sum(x, axes):
    for axis in axes:
        count = lax.axis_size(axis)
        if count & (count - 1):
            x = lax.psum(x, axis)
            continue
        step = 1
        while step < count:
            x = x + lax.ppermute(x, axis, [(i, i ^ step) for i in range(count)])
            step *= 2
    return x


def local(residual, points, noise, block_list):
    part = lax.axis_index("rhs")
    pairs = lax.axis_size("rhs")
    blk_count = lax.axis_size("blk")
    own = residual[:, 0]
    own_points = points[:, 0]
    length = own.shape[1]
    half = length // pairs
    rim = REACH * BS
    inner = length - rim
    ring_axes = ("blk", "rhs")

    def at(b, j):
        return (b % blk_count) * pairs + j

    same_side = [(at(b, 0), at(b + 1, 0)) for b in range(blk_count)]
    same_side += [(at(b, 1), at(b - 1, 1)) for b in range(blk_count)]
    cross_side = [(at(b, 1), at(b + 1, 0)) for b in range(blk_count)]
    cross_side += [(at(b, 0), at(b - 1, 1)) for b in range(blk_count)]
    from_partner = swap_pair(lax.dynamic_slice_in_dim(own, (1 - part) * rim, inner, 1), part)
    edge_at = (1 - part) * inner
    edge = jnp.concatenate(
        [
            lax.dynamic_slice_in_dim(own, edge_at, rim, 1),
            lax.dynamic_slice_in_dim(own_points, edge_at, rim, 1),
        ],
        axis=0,
    )
    from_same = lax.ppermute(edge, ring_axes, same_side)
    from_cross = lax.ppermute(
        lax.dynamic_slice_in_dim(own, part * inner, rim, 1), ring_axes, cross_side
    )
    sides_here = own.shape[0]
    mine_wide = lax.dynamic_slice_in_dim(own, part * rim, inner, 1)
    points_wide = lax.dynamic_slice_in_dim(own_points, part * rim, inner, 1)
    same_field = from_same[:sides_here]
    same_points = from_same[sides_here:]
    low_first = jnp.concatenate(
        [jnp.concatenate([same_field, mine_wide], 1), jnp.concatenate([from_cross, from_partner], 1)], 0
    )
    high_first = jnp.concatenate(
        [jnp.concatenate([from_partner, from_cross], 1), jnp.concatenate([mine_wide, same_field], 1)], 0
    )
    first_wide = jnp.where(part == 0, low_first, high_first)
    coords_wide = jnp.where(
        part == 0,
        jnp.concatenate([same_points, points_wide], 1),
        jnp.concatenate([points_wide, same_points], 1),
    )
    field = first_wide[:, rim : rim + half]
    nugget = lax.dynamic_slice_in_dim(noise[0], part * half, half, 0)
    own_blocks = half // BS
    ring = lax.axis_size("blk") * pairs
    first_block = (lax.axis_index("blk") * pairs + part) * own_blocks
    listed = block_list[0].astype(jnp.float32)
    nine = jnp.concatenate(
        [listed[:REACH], jnp.ones((1, listed.shape[1]), jnp.float32), listed[REACH:]], axis=0
    )
    margin = S * REACH
    wrapped = jnp.concatenate([nine[:, -margin:], nine, nine[:, :margin]], axis=1)
    powers = [field]
    own_weights = lax.dynamic_slice_in_dim(wrapped, first_block + margin, own_blocks, 1)
    tiles = lax.optimization_barrier(band_tiles(coords_wide, own_weights, own_blocks))
    current = field
    for power_step in range(S):
        widened = first_wide if power_step == 0 else extended(current, ("blk", "rhs"), ring, rim)
        current = band_product(widened, tiles, own_blocks) + (nugget - centre_shift) * current
        powers.append(current)
    flat = jnp.concatenate(powers, axis=0)
    count_points = half * ring * lax.axis_size("leaf")
    gram = butterfly_sum(row_products(flat[: S * M], flat), ("leaf", "blk", "rhs"))
    inverse_low, combo = galerkin(gram, count_points, M)
    first_rows = flat[: S * M]
    image = flat[M:] + centre_shift * first_rows
    correction = jnp.dot(combo, first_rows, precision=exact)
    new_residual = field - jnp.dot(combo, image, precision=exact)
    basis = jnp.dot(inverse_low, first_rows, precision=exact)
    results = []
    for full in (correction, new_residual, basis):
        groups = full.reshape(pairs, -1, half)
        keep = lax.dynamic_index_in_dim(groups, part, 0, False)
        give = lax.dynamic_index_in_dim(groups, 1 - part, 0, False)
        results.append(in_order(keep, swap_pair(give, part), part, 1)[:, None])
    return tuple(results)


def solution(mesh):
    placed = (
        P("rhs", "leaf", "blk"),
        P(None, "leaf", "blk"),
        P("leaf", "blk"),
        P("leaf", None, None),
    )
    return jax.shard_map(
        local,
        mesh=mesh,
        in_specs=placed,
        out_specs=(P("rhs", "leaf", "blk"), P("rhs", "leaf", "blk"), P("rhs", "leaf", "blk")),
        check_vma=False,
    )
```

```python
import jax
import jax.numpy as jnp
from jax import lax
from jax.sharding import PartitionSpec as P

M = 32
S = 4
BS = 256
REACH = 4
SUPPORT = 1408


centre_shift = 1.5
amplitude = 1.1
exact = lax.Precision.HIGHEST


def extended(x, axes, count, width):
    length = x.shape[1]
    up = [(i, (i + 1) % count) for i in range(count)]
    down = [(j, i) for i, j in up]
    before = lax.ppermute(x[:, length - width :], axes, up)
    after = lax.ppermute(x[:, :width], axes, down)
    return jnp.concatenate([before, x, after], axis=1)


def swap_pair(x, part):
    return lax.ppermute(x, "rhs", [(0, 1), (1, 0)])


def in_order(mine, other, part, axis):
    first = jnp.concatenate([mine, other], axis=axis)
    second = jnp.concatenate([other, mine], axis=axis)
    return jnp.where(part == 0, first, second)


def kernel_tile(near_points, own_points):
    squared = (near_points[0][:, None] - own_points[0][None, :]) ** 2
    squared = squared + (near_points[1][:, None] - own_points[1][None, :]) ** 2
    squared = squared + (near_points[2][:, None] - own_points[2][None, :]) ** 2
    radius = jnp.sqrt(squared) / SUPPORT
    remain = jnp.maximum(1.0 - radius, 0.0)
    return remain * remain * (remain * remain) * (4.0 * radius + 1.0) * (amplitude / SUPPORT)


def band_tiles(points_wide, weights, rows_out):
    width = 2 * REACH + 1
    blocks = points_wide.reshape(3, -1, BS)
    own = blocks[:, REACH : REACH + rows_out]
    near = jnp.stack([blocks[:, k : k + rows_out] for k in range(width)], axis=2)
    tiles = jax.vmap(jax.vmap(kernel_tile, in_axes=(1, None)), in_axes=(1, 1))(near, own)
    return tiles * jnp.transpose(weights)[:, :, None, None]


def band_product(field_wide, tiles, rows_out):
    width = 2 * REACH + 1
    count = field_wide.shape[0]
    blocks = field_wide.reshape(count, -1, BS)
    near = jnp.stack([blocks[:, k : k + rows_out] for k in range(width)], axis=2)
    out = jnp.einsum("mbkq,bkqp->mbp", near, tiles, precision=exact)
    return out.reshape(count, rows_out * BS)


def galerkin(gram, count_points, count_sides):
    normed = gram / count_points
    basis_count = normed.shape[0]
    gram_basis = normed[:basis_count, :basis_count]
    factor_low = jnp.linalg.cholesky(gram_basis)
    inverse_low = lax.linalg.triangular_solve(
        factor_low, jnp.eye(basis_count, dtype=jnp.float32), left_side=True, lower=True
    )
    cross = normed[:basis_count, count_sides:] + centre_shift * gram_basis
    projected = jnp.dot(
        jnp.dot(inverse_low, cross, precision=exact), inverse_low.T, precision=exact
    )
    projected = 0.5 * (projected + projected.T)
    small_side = jnp.dot(inverse_low, gram_basis[:, :count_sides], precision=exact)
    proj_factor = jnp.linalg.cholesky(projected)
    halfway = lax.linalg.triangular_solve(proj_factor, small_side, left_side=True, lower=True)
    coeffs = lax.linalg.triangular_solve(
        proj_factor, halfway, left_side=True, lower=True, transpose_a=True
    )
    combo = jnp.dot(coeffs.T, inverse_low, precision=exact)
    return (inverse_low, combo)


def row_products(rows, cols):
    return lax.dot_general(rows, cols, (((1,), (1,)), ((), ())), precision=exact)


def butterfly_sum(x, axes):
    for axis in axes:
        count = lax.axis_size(axis)
        if count & (count - 1):
            x = lax.psum(x, axis)
            continue
        step = 1
        while step < count:
            x = x + lax.ppermute(x, axis, [(i, i ^ step) for i in range(count)])
            step *= 2
    return x


def local(residual, points, noise, block_list):
    part = lax.axis_index("rhs")
    pairs = lax.axis_size("rhs")
    blk_count = lax.axis_size("blk")
    own = residual[:, 0]
    own_points = points[:, 0]
    length = own.shape[1]
    half = length // pairs
    rim = REACH * BS
    inner = length - rim
    ring_axes = ("blk", "rhs")

    def at(b, j):
        return (b % blk_count) * pairs + j

    same_side = [(at(b, 0), at(b + 1, 0)) for b in range(blk_count)]
    same_side += [(at(b, 1), at(b - 1, 1)) for b in range(blk_count)]
    cross_side = [(at(b, 1), at(b + 1, 0)) for b in range(blk_count)]
    cross_side += [(at(b, 0), at(b - 1, 1)) for b in range(blk_count)]
    from_partner = swap_pair(lax.dynamic_slice_in_dim(own, (1 - part) * rim, inner, 1), part)
    edge_at = (1 - part) * inner
    edge = jnp.concatenate(
        [
            lax.dynamic_slice_in_dim(own, edge_at, rim, 1),
            lax.dynamic_slice_in_dim(own_points, edge_at, rim, 1),
        ],
        axis=0,
    )
    from_same = lax.ppermute(edge, ring_axes, same_side)
    from_cross = lax.ppermute(
        lax.dynamic_slice_in_dim(own, part * inner, rim, 1), ring_axes, cross_side
    )
    sides_here = own.shape[0]
    mine_wide = lax.dynamic_slice_in_dim(own, part * rim, inner, 1)
    points_wide = lax.dynamic_slice_in_dim(own_points, part * rim, inner, 1)
    same_field = from_same[:sides_here]
    same_points = from_same[sides_here:]
    low_first = jnp.concatenate(
        [jnp.concatenate([same_field, mine_wide], 1), jnp.concatenate([from_cross, from_partner], 1)], 0
    )
    high_first = jnp.concatenate(
        [jnp.concatenate([from_partner, from_cross], 1), jnp.concatenate([mine_wide, same_field], 1)], 0
    )
    first_wide = jnp.where(part == 0, low_first, high_first)
    coords_wide = jnp.where(
        part == 0,
        jnp.concatenate([same_points, points_wide], 1),
        jnp.concatenate([points_wide, same_points], 1),
    )
    field = first_wide[:, rim : rim + half]
    nugget = lax.dynamic_slice_in_dim(noise[0], part * half, half, 0)
    own_blocks = half // BS
    ring = lax.axis_size("blk") * pairs
    first_block = (lax.axis_index("blk") * pairs + part) * own_blocks
    listed = block_list[0].astype(jnp.float32)
    nine = jnp.concatenate(
        [listed[:REACH], jnp.ones((1, listed.shape[1]), jnp.float32), listed[REACH:]], axis=0
    )
    margin = S * REACH
    wrapped = jnp.concatenate([nine[:, -margin:], nine, nine[:, :margin]], axis=1)
    powers = [field]
    own_weights = lax.dynamic_slice_in_dim(wrapped, first_block + margin, own_blocks, 1)
    tiles = lax.optimization_barrier(band_tiles(coords_wide, own_weights, own_blocks))
    shift = nugget - centre_shift
    current = band_product(first_wide, tiles, own_blocks) + shift * field
    stacked = jnp.zeros((S,) + field.shape, field.dtype).at[0].set(current)

    def power_step(index, carry):
        stacked, current = carry
        widened = extended(current, ("blk", "rhs"), ring, rim)
        current = band_product(widened, tiles, own_blocks) + shift * current
        return (lax.dynamic_update_index_in_dim(stacked, current, index, 0), current)

    stacked, current = lax.fori_loop(1, S, power_step, (stacked, current))
    powers = [field] + [stacked[k] for k in range(S)]
    flat = jnp.concatenate(powers, axis=0)
    count_points = half * ring * lax.axis_size("leaf")
    gram = butterfly_sum(row_products(flat[: S * M], flat), ("leaf", "blk", "rhs"))
    inverse_low, combo = galerkin(gram, count_points, M)
    first_rows = flat[: S * M]
    image = flat[M:] + centre_shift * first_rows
    correction = jnp.dot(combo, first_rows, precision=exact)
    new_residual = field - jnp.dot(combo, image, precision=exact)
    basis = jnp.dot(inverse_low, first_rows, precision=exact)
    results = []
    for full in (correction, new_residual, basis):
        groups = full.reshape(pairs, -1, half)
        keep = lax.dynamic_index_in_dim(groups, part, 0, False)
        give = lax.dynamic_index_in_dim(groups, 1 - part, 0, False)
        results.append(in_order(keep, swap_pair(give, part), part, 1)[:, None])
    return tuple(results)


def solution(mesh):
    placed = (
        P("rhs", "leaf", "blk"),
        P(None, "leaf", "blk"),
        P("leaf", "blk"),
        P("leaf", None, None),
    )
    return jax.shard_map(
        local,
        mesh=mesh,
        in_specs=placed,
        out_specs=(P("rhs", "leaf", "blk"), P("rhs", "leaf", "blk"), P("rhs", "leaf", "blk")),
        check_vma=False,
    )
```

```python
import jax
import jax.numpy as jnp
from jax import lax
from jax.sharding import PartitionSpec as P

M = 32
S = 4
BS = 256
REACH = 4
SUPPORT = 1408


centre_shift = 1.5
amplitude = 1.1
exact = lax.Precision.HIGHEST


def extended(x, axes, count, width):
    length = x.shape[1]
    up = [(i, (i + 1) % count) for i in range(count)]
    down = [(j, i) for i, j in up]
    before = lax.ppermute(x[:, length - width :], axes, up)
    after = lax.ppermute(x[:, :width], axes, down)
    return jnp.concatenate([before, x, after], axis=1)


def swap_pair(x, part):
    return lax.ppermute(x, "rhs", [(0, 1), (1, 0)])


def in_order(mine, other, part, axis):
    first = jnp.concatenate([mine, other], axis=axis)
    second = jnp.concatenate([other, mine], axis=axis)
    return jnp.where(part == 0, first, second)


def kernel_tile(near_points, own_points):
    squared = (near_points[0][:, None] - own_points[0][None, :]) ** 2
    squared = squared + (near_points[1][:, None] - own_points[1][None, :]) ** 2
    squared = squared + (near_points[2][:, None] - own_points[2][None, :]) ** 2
    radius = jnp.sqrt(squared) / SUPPORT
    remain = jnp.maximum(1.0 - radius, 0.0)
    return remain * remain * (remain * remain) * (4.0 * radius + 1.0) * (amplitude / SUPPORT)


def band_tiles(points_wide, weights, rows_out):
    width = 2 * REACH + 1
    blocks = points_wide.reshape(3, -1, BS)
    own = blocks[:, REACH : REACH + rows_out]
    near = jnp.stack([blocks[:, k : k + rows_out] for k in range(width)], axis=2)
    tiles = jax.vmap(jax.vmap(kernel_tile, in_axes=(1, None)), in_axes=(1, 1))(near, own)
    return tiles * jnp.transpose(weights)[:, :, None, None]


def band_product(field_wide, tiles, rows_out):
    width = 2 * REACH + 1
    count = field_wide.shape[0]
    blocks = field_wide.reshape(count, -1, BS)
    near = jnp.stack([blocks[:, k : k + rows_out] for k in range(width)], axis=2)
    out = jnp.einsum("mbkq,bkqp->mbp", near, tiles, precision=exact)
    return out.reshape(count, rows_out * BS)


def galerkin(gram, count_points, count_sides):
    normed = gram / count_points
    basis_count = normed.shape[0]
    gram_basis = normed[:basis_count, :basis_count]
    factor_low = jnp.linalg.cholesky(gram_basis)
    inverse_low = lax.linalg.triangular_solve(
        factor_low, jnp.eye(basis_count, dtype=jnp.float32), left_side=True, lower=True
    )
    cross = normed[:basis_count, count_sides:] + centre_shift * gram_basis
    projected = jnp.dot(
        jnp.dot(inverse_low, cross, precision=exact), inverse_low.T, precision=exact
    )
    projected = 0.5 * (projected + projected.T)
    small_side = jnp.dot(inverse_low, gram_basis[:, :count_sides], precision=exact)
    proj_factor = jnp.linalg.cholesky(projected)
    halfway = lax.linalg.triangular_solve(proj_factor, small_side, left_side=True, lower=True)
    coeffs = lax.linalg.triangular_solve(
        proj_factor, halfway, left_side=True, lower=True, transpose_a=True
    )
    combo = jnp.dot(coeffs.T, inverse_low, precision=exact)
    return (inverse_low, combo)


def row_products(rows, cols):
    return lax.dot_general(rows, cols, (((1,), (1,)), ((), ())), precision=exact)


def butterfly_sum(x, axes):
    for axis in axes:
        count = lax.axis_size(axis)
        if count & (count - 1):
            x = lax.psum(x, axis)
            continue
        step = 1
        while step < count:
            x = x + lax.ppermute(x, axis, [(i, i ^ step) for i in range(count)])
            step *= 2
    return x


def local(residual, points, noise, block_list):
    part = lax.axis_index("rhs")
    pairs = lax.axis_size("rhs")
    blk_count = lax.axis_size("blk")
    own = residual[:, 0]
    own_points = points[:, 0]
    length = own.shape[1]
    half = length // pairs
    rim = REACH * BS
    inner = length - rim
    ring_axes = ("blk", "rhs")

    def at(b, j):
        return (b % blk_count) * pairs + j

    same_side = [(at(b, 0), at(b + 1, 0)) for b in range(blk_count)]
    same_side += [(at(b, 1), at(b - 1, 1)) for b in range(blk_count)]
    cross_side = [(at(b, 1), at(b + 1, 0)) for b in range(blk_count)]
    cross_side += [(at(b, 0), at(b - 1, 1)) for b in range(blk_count)]
    from_partner = swap_pair(lax.dynamic_slice_in_dim(own, (1 - part) * rim, inner, 1), part)
    edge_at = (1 - part) * inner
    edge = jnp.concatenate(
        [
            lax.dynamic_slice_in_dim(own, edge_at, rim, 1),
            lax.dynamic_slice_in_dim(own_points, edge_at, rim, 1),
        ],
        axis=0,
    )
    from_same = lax.ppermute(edge, ring_axes, same_side)
    from_cross = lax.ppermute(
        lax.dynamic_slice_in_dim(own, part * inner, rim, 1), ring_axes, cross_side
    )
    sides_here = own.shape[0]
    mine_wide = lax.dynamic_slice_in_dim(own, part * rim, inner, 1)
    points_wide = lax.dynamic_slice_in_dim(own_points, part * rim, inner, 1)
    same_field = from_same[:sides_here]
    same_points = from_same[sides_here:]
    low_first = jnp.concatenate(
        [jnp.concatenate([same_field, mine_wide], 1), jnp.concatenate([from_cross, from_partner], 1)], 0
    )
    high_first = jnp.concatenate(
        [jnp.concatenate([from_partner, from_cross], 1), jnp.concatenate([mine_wide, same_field], 1)], 0
    )
    first_wide = jnp.where(part == 0, low_first, high_first)
    coords_wide = jnp.where(
        part == 0,
        jnp.concatenate([same_points, points_wide], 1),
        jnp.concatenate([points_wide, same_points], 1),
    )
    field = first_wide[:, rim : rim + half]
    nugget = lax.dynamic_slice_in_dim(noise[0], part * half, half, 0)
    own_blocks = half // BS
    ring = lax.axis_size("blk") * pairs
    first_block = (lax.axis_index("blk") * pairs + part) * own_blocks
    listed = block_list[0].astype(jnp.float32)
    nine = jnp.concatenate(
        [listed[:REACH], jnp.ones((1, listed.shape[1]), jnp.float32), listed[REACH:]], axis=0
    )
    margin = S * REACH
    wrapped = jnp.concatenate([nine[:, -margin:], nine, nine[:, :margin]], axis=1)
    powers = [field]
    own_weights = lax.dynamic_slice_in_dim(wrapped, first_block + margin, own_blocks, 1)
    tiles = lax.optimization_barrier(band_tiles(coords_wide, own_weights, own_blocks))
    current = field
    for power_step in range(S):
        widened = first_wide if power_step == 0 else extended(current, ("blk", "rhs"), ring, rim)
        current = band_product(widened, tiles, own_blocks) + (nugget - centre_shift) * current
        powers.append(current)
    flat = jnp.concatenate(powers, axis=0)
    count_points = half * ring * lax.axis_size("leaf")
    gram = butterfly_sum(row_products(flat[: S * M], flat), ("leaf", "blk", "rhs"))
    inverse_low, combo = galerkin(gram, count_points, M)
    first_rows = flat[: S * M]
    image = flat[M:] + centre_shift * first_rows
    correction = jnp.dot(combo, first_rows, precision=exact)
    new_residual = field - jnp.dot(combo, image, precision=exact)
    basis = jnp.dot(inverse_low, first_rows, precision=exact)
    kept, given = [], []
    for full in (correction, new_residual, basis):
        groups = full.reshape(pairs, -1, half)
        kept.append(lax.dynamic_index_in_dim(groups, part, 0, False))
        given.append(lax.dynamic_index_in_dim(groups, 1 - part, 0, False))
    got = swap_pair(jnp.concatenate(given, axis=0), part)
    joined = in_order(jnp.concatenate(kept, axis=0), got, part, 1)
    results = []
    start = 0
    for piece in kept:
        results.append(joined[start : start + piece.shape[0], None])
        start += piece.shape[0]
    return tuple(results)


def solution(mesh):
    placed = (
        P("rhs", "leaf", "blk"),
        P(None, "leaf", "blk"),
        P("leaf", "blk"),
        P("leaf", None, None),
    )
    return jax.shard_map(
        local,
        mesh=mesh,
        in_specs=placed,
        out_specs=(P("rhs", "leaf", "blk"), P("rhs", "leaf", "blk"), P("rhs", "leaf", "blk")),
        check_vma=False,
    )
```

```python
import jax
import jax.numpy as jnp
from jax import lax
from jax.sharding import PartitionSpec as P

M = 32
S = 4
BS = 256
REACH = 4
SUPPORT = 1408


centre_shift = 1.5
amplitude = 1.1
exact = lax.Precision.HIGHEST


def extended(x, axes, count, width):
    length = x.shape[1]
    up = [(i, (i + 1) % count) for i in range(count)]
    down = [(j, i) for i, j in up]
    before = lax.ppermute(x[:, length - width :], axes, up)
    after = lax.ppermute(x[:, :width], axes, down)
    return jnp.concatenate([before, x, after], axis=1)


def swap_pair(x, part):
    return lax.ppermute(x, "rhs", [(0, 1), (1, 0)])


def in_order(mine, other, part, axis):
    first = jnp.concatenate([mine, other], axis=axis)
    second = jnp.concatenate([other, mine], axis=axis)
    return jnp.where(part == 0, first, second)


def kernel_tile(near_points, own_points):
    squared = (near_points[0][:, None] - own_points[0][None, :]) ** 2
    squared = squared + (near_points[1][:, None] - own_points[1][None, :]) ** 2
    squared = squared + (near_points[2][:, None] - own_points[2][None, :]) ** 2
    radius = jnp.sqrt(squared) / SUPPORT
    remain = jnp.maximum(1.0 - radius, 0.0)
    return remain * remain * (remain * remain) * (4.0 * radius + 1.0) * (amplitude / SUPPORT)


def band_tiles(points_wide, weights, rows_out):
    width = 2 * REACH + 1
    blocks = points_wide.reshape(3, -1, BS)
    own = blocks[:, REACH : REACH + rows_out]
    near = jnp.stack([blocks[:, k : k + rows_out] for k in range(width)], axis=2)
    tiles = jax.vmap(jax.vmap(kernel_tile, in_axes=(1, None)), in_axes=(1, 1))(near, own)
    return tiles * jnp.transpose(weights)[:, :, None, None]


def band_product(field_wide, tiles, rows_out):
    width = 2 * REACH + 1
    count = field_wide.shape[0]
    blocks = field_wide.reshape(count, -1, BS)
    near = jnp.stack([blocks[:, k : k + rows_out] for k in range(width)], axis=2)
    out = jnp.einsum("mbkq,bkqp->mbp", near, tiles, precision=exact)
    return out.reshape(count, rows_out * BS)


def galerkin(gram, count_points, count_sides):
    normed = gram / count_points
    basis_count = normed.shape[0]
    gram_basis = normed[:basis_count, :basis_count]
    factor_low = jnp.linalg.cholesky(gram_basis)
    inverse_low = lax.linalg.triangular_solve(
        factor_low, jnp.eye(basis_count, dtype=jnp.float32), left_side=True, lower=True
    )
    cross = normed[:basis_count, count_sides:] + centre_shift * gram_basis
    projected = jnp.dot(
        jnp.dot(inverse_low, cross, precision=exact), inverse_low.T, precision=exact
    )
    projected = 0.5 * (projected + projected.T)
    small_side = jnp.dot(inverse_low, gram_basis[:, :count_sides], precision=exact)
    proj_factor = jnp.linalg.cholesky(projected)
    halfway = lax.linalg.triangular_solve(proj_factor, small_side, left_side=True, lower=True)
    coeffs = lax.linalg.triangular_solve(
        proj_factor, halfway, left_side=True, lower=True, transpose_a=True
    )
    combo = jnp.dot(coeffs.T, inverse_low, precision=exact)
    return (inverse_low, combo)


def row_products(rows, cols):
    return lax.dot_general(rows, cols, (((1,), (1,)), ((), ())), precision=exact)


def butterfly_sum(x, axes):
    for axis in axes:
        count = lax.axis_size(axis)
        if count & (count - 1):
            x = lax.psum(x, axis)
            continue
        step = 1
        while step < count:
            x = x + lax.ppermute(x, axis, [(i, i ^ step) for i in range(count)])
            step *= 2
    return x


def local(residual, points, noise, block_list):
    part = lax.axis_index("rhs")
    pairs = lax.axis_size("rhs")
    blk_count = lax.axis_size("blk")
    own = residual[:, 0]
    own_points = points[:, 0]
    length = own.shape[1]
    half = length // pairs
    rim = REACH * BS
    inner = length - rim
    ring_axes = ("blk", "rhs")

    def at(b, j):
        return (b % blk_count) * pairs + j

    same_side = [(at(b, 0), at(b + 1, 0)) for b in range(blk_count)]
    same_side += [(at(b, 1), at(b - 1, 1)) for b in range(blk_count)]
    cross_side = [(at(b, 1), at(b + 1, 0)) for b in range(blk_count)]
    cross_side += [(at(b, 0), at(b - 1, 1)) for b in range(blk_count)]
    from_partner = swap_pair(lax.dynamic_slice_in_dim(own, (1 - part) * rim, inner, 1), part)
    edge_at = (1 - part) * inner
    edge = jnp.concatenate(
        [
            lax.dynamic_slice_in_dim(own, edge_at, rim, 1),
            lax.dynamic_slice_in_dim(own_points, edge_at, rim, 1),
        ],
        axis=0,
    )
    from_same = lax.ppermute(edge, ring_axes, same_side)
    from_cross = lax.ppermute(
        lax.dynamic_slice_in_dim(own, part * inner, rim, 1), ring_axes, cross_side
    )
    sides_here = own.shape[0]
    mine_wide = lax.dynamic_slice_in_dim(own, part * rim, inner, 1)
    points_wide = lax.dynamic_slice_in_dim(own_points, part * rim, inner, 1)
    same_field = from_same[:sides_here]
    same_points = from_same[sides_here:]
    low_first = jnp.concatenate(
        [jnp.concatenate([same_field, mine_wide], 1), jnp.concatenate([from_cross, from_partner], 1)], 0
    )
    high_first = jnp.concatenate(
        [jnp.concatenate([from_partner, from_cross], 1), jnp.concatenate([mine_wide, same_field], 1)], 0
    )
    first_wide = jnp.where(part == 0, low_first, high_first)
    coords_wide = jnp.where(
        part == 0,
        jnp.concatenate([same_points, points_wide], 1),
        jnp.concatenate([points_wide, same_points], 1),
    )
    field = first_wide[:, rim : rim + half]
    nugget = lax.dynamic_slice_in_dim(noise[0], part * half, half, 0)
    own_blocks = half // BS
    ring = lax.axis_size("blk") * pairs
    first_block = (lax.axis_index("blk") * pairs + part) * own_blocks
    listed = block_list[0].astype(jnp.float32)
    nine = jnp.concatenate(
        [listed[:REACH], jnp.ones((1, listed.shape[1]), jnp.float32), listed[REACH:]], axis=0
    )
    margin = S * REACH
    wrapped = jnp.concatenate([nine[:, -margin:], nine, nine[:, :margin]], axis=1)
    powers = [field]
    own_weights = lax.dynamic_slice_in_dim(wrapped, first_block + margin, own_blocks, 1)
    tiles = lax.optimization_barrier(band_tiles(coords_wide, own_weights, own_blocks))
    current = field
    for power_step in range(S):
        widened = first_wide if power_step == 0 else extended(current, ("blk", "rhs"), ring, rim)
        if power_step == S - 1:
            basis_rows = jnp.concatenate(powers, axis=0)
            gram_basis_part = row_products(basis_rows, basis_rows)
        current = band_product(widened, tiles, own_blocks) + (nugget - centre_shift) * current
        powers.append(current)
    flat = jnp.concatenate(powers, axis=0)
    count_points = half * ring * lax.axis_size("leaf")
    gram_part = jnp.concatenate([gram_basis_part, row_products(basis_rows, current)], axis=1)
    gram = butterfly_sum(gram_part, ("leaf", "blk", "rhs"))
    inverse_low, combo = galerkin(gram, count_points, M)
    first_rows = flat[: S * M]
    image = flat[M:] + centre_shift * first_rows
    correction = jnp.dot(combo, first_rows, precision=exact)
    new_residual = field - jnp.dot(combo, image, precision=exact)
    basis = jnp.dot(inverse_low, first_rows, precision=exact)
    results = []
    for full in (correction, new_residual, basis):
        groups = full.reshape(pairs, -1, half)
        keep = lax.dynamic_index_in_dim(groups, part, 0, False)
        give = lax.dynamic_index_in_dim(groups, 1 - part, 0, False)
        results.append(in_order(keep, swap_pair(give, part), part, 1)[:, None])
    return tuple(results)


def solution(mesh):
    placed = (
        P("rhs", "leaf", "blk"),
        P(None, "leaf", "blk"),
        P("leaf", "blk"),
        P("leaf", None, None),
    )
    return jax.shard_map(
        local,
        mesh=mesh,
        in_specs=placed,
        out_specs=(P("rhs", "leaf", "blk"), P("rhs", "leaf", "blk"), P("rhs", "leaf", "blk")),
        check_vma=False,
    )
```
